256 devices in a mesh: tm: 32 (over x_lo, z, core), strip: 8 (over x_hi, y).
Axes of the slice: x: 4 (x_hi: 2, x_lo: 2; x = x_hi * 2 + x_lo), y: 4, z: 8, core: 2. Of those that a mesh axis runs over, the one named last changes fastest.
Arguments:
- movie: bfloat16 [4096, 65536], P('tm', 'strip'), may hold values from -6 to 6
- shifts: float32 [4096, 128], P('tm', 'strip'), may hold values from -1 to 1
- projection: bfloat16 [65536, 256], P('strip'), may hold values from -0.03125 to 0.03125
- footprints: bfloat16 [256, 65536], P(None, 'strip'), may hold values from -0.375 to 0.375
- quality: float32 [4096], replicated, may hold values from 0.1 to 1
- continuity: float32 [4096], replicated, may hold values from 0.5 to 1
- retention: float32 [256], replicated, may hold values from 0.9 to 1, as said below
Outputs:
- activity: float32 [256, 4096], P('strip', 'tm')
- residual: bfloat16 [4096, 65536], P('tm', 'strip')
The draws below stay inside these ranges and needn't reach their ends.
Inputs may be any that keep to these rules, and one draw needn't show every extreme that they name: `retention`: each factor's kernel weight falls by this factor from one frame to the next, times continuity.
All inputs are finite; a program needn't handle non-finite values.
Results may differ from the reference program's by a relative error of at most 0.0053.
Values may be sent and summed in bfloat16 or wider, within the bound.
A program may use at most 128 MiB of HBM per device.

```python
import math
import jax
import jax.numpy as jnp
from jax import lax

FRAMES_DEV = 128
COLUMNS = 512
FACTORS = 256
RADIUS = 1
FRAMES = 4096
ROWS = 128


def draw_retention(key, part):
    seeded = jax.random.fold_in(key, 101)
    pick_key, slow_key, fast_key = jax.random.split(seeded, 3)
    slow_share = 5
    slow_pick = jax.random.randint(pick_key, (FACTORS,), 0, 10) < slow_share
    border = 3.0 / FRAMES
    slow_rate = jnp.exp(jax.random.uniform(slow_key, (FACTORS,), jnp.float32, jnp.log(0.25 / FRAMES), jnp.log(border)))
    fast_rate = jnp.exp(jax.random.uniform(fast_key, (FACTORS,), jnp.float32, jnp.log(border), jnp.log(0.1)))
    return (1.0 - jnp.where(slow_pick, slow_rate, fast_rate)).astype(jnp.float32)


def draw_continuity(key, part):
    seeded = jax.random.fold_in(key, 202)
    place_key, level_key = jax.random.split(seeded, 2)
    places = jax.random.randint(place_key, (4,), 0, FRAMES)
    levels = jax.random.uniform(level_key, (4,), jnp.float32, 0.5, 0.8)
    frame_ids = jnp.arange(FRAMES)
    matches = frame_ids[:, None] == places[None, :]
    return jnp.min(jnp.where(matches, levels[None, :], 1.0), axis=1).astype(jnp.float32)


def strengthened(values, rng, source, target, parts, factor):
    owner, partner = [(jnp.arange(values.shape[dim]) // (values.shape[dim] // parts)).reshape([-1 if axis == dim else 1 for axis in range(values.ndim)]) for dim in (source, target)]
    chosen = jax.random.permutation(rng, parts)[partner]
    strong = (owner == chosen) | (owner == (partner + parts // 2) % parts)
    return jnp.where(strong, factor * values, values)


def block_scale(stream_key, dims, pieces, low, high):
    def one(dim, blocks):
        heights = jax.random.uniform(jax.random.fold_in(jax.random.fold_in(stream_key, 6), dim), (blocks,), jnp.float32, low / len(pieces), high / len(pieces))
        return jnp.repeat(jnp.exp(heights), dims[dim] // blocks).reshape((-1,) + (1,) * (len(dims) - dim - 1))

    gain = one(*pieces[0])
    for cut in pieces[1:]:
        gain = gain * one(*cut)
    return gain


def gaussian(own_key, dims, scale, most, cuts=(), dtype=jnp.bfloat16):
    array = scale * jax.random.normal(own_key, dims, jnp.float32)
    if cuts:
        array = array * block_scale(own_key, dims, cuts, -0.22, 0.18)
    return jnp.clip(array, -most, most).astype(dtype)


def gaussian_with(key, extent, scale, bound, cuts, heavy, kind=jnp.bfloat16):
    result = scale * jax.random.normal(key, extent, jnp.float32)
    if cuts:
        result = result * block_scale(key, extent, cuts, -0.22, 0.18)
    return jnp.clip(strengthened(result, jax.random.fold_in(key, 3), *heavy), -bound, bound).astype(kind)


def setup_inputs(seed: int = 0) -> dict:
    arg_keys = jax.random.split(jax.random.key(seed), 8)
    return {
        "movie": gaussian(arg_keys[0], (FRAMES, ROWS * COLUMNS), 1.0, 6.0, ((0, 32), (1, 8))),
        "shifts": jnp.clip(jax.random.uniform(arg_keys[1], (FRAMES, ROWS), jnp.float32, -1.0, 1.0) * block_scale(arg_keys[1], (FRAMES, ROWS), ((0, 32), (1, 8)), -0.4, 0.0), -1.0, 1.0),
        "projection": gaussian_with(arg_keys[2], (ROWS * COLUMNS, FACTORS), (ROWS * COLUMNS) ** -0.5, 0.03125, ((0, 8),), (0, 1, 8, 2.0)),
        "footprints": gaussian(arg_keys[3], (FACTORS, ROWS * COLUMNS), FACTORS ** -0.5, 0.375, ((1, 8),)),
        "quality": jnp.clip(jnp.exp(jax.random.uniform(arg_keys[4], (FRAMES,), jnp.float32, math.log(0.1), math.log(1.0))), 0.1, 1.0),
        "continuity": draw_continuity(jax.random.fold_in(arg_keys[7], 71), 0),
        "retention": draw_retention(jax.random.fold_in(arg_keys[7], 71), 0),
    }


def warp_block(movie_block, shift_block):
    padded = jnp.pad(movie_block, ((0, 0), (RADIUS * COLUMNS, RADIUS * COLUMNS)))
    summed = jnp.zeros(movie_block.shape, jnp.float32)
    for offset in range(-RADIUS, RADIUS + 1):
        weight = jnp.maximum(0.0, 1.0 - jnp.abs(shift_block - offset))
        spread = jnp.repeat(weight, COLUMNS, axis=1)
        begin = (RADIUS + offset) * COLUMNS
        window = padded[:, begin:begin + ROWS * COLUMNS].astype(jnp.float32)
        summed = summed + spread * window
    return summed.astype(jnp.bfloat16)

def forward_step(carried, inputs):
    new_sum = inputs[0] * carried[0] + inputs[1]
    new_norm = inputs[0] * carried[1] + inputs[2]
    return ((new_sum, new_norm), (new_sum, new_norm))

def backward_step(carried, inputs):
    new_sum = inputs[0] * (carried[0] + inputs[1])
    new_norm = inputs[0] * (carried[1] + inputs[2])
    return ((new_sum, new_norm), (new_sum, new_norm))

def reference(movie, shifts, projection, footprints, quality, continuity, retention):
    blocks = FRAMES // FRAMES_DEV
    movie_blocks = movie.reshape(blocks, FRAMES_DEV, ROWS * COLUMNS)
    shift_blocks = shifts.reshape(blocks, FRAMES_DEV, ROWS)

    def project(pair):
        warped = warp_block(pair[0], pair[1])
        return jnp.dot(warped, projection, preferred_element_type=jnp.float32)
    traces = lax.map(project, (movie_blocks, shift_blocks)).reshape(FRAMES, FACTORS)
    transition = continuity[:, None] * retention[None, :]
    weighted = quality[:, None] * traces
    quality_cols = jnp.broadcast_to(quality[:, None], (FRAMES, FACTORS))
    zero_row = jnp.zeros((FACTORS,), jnp.float32)
    unused, ahead = lax.scan(forward_step, (zero_row, zero_row), (transition, weighted, quality_cols))
    unused, behind = lax.scan(backward_step, (zero_row, zero_row), (transition, weighted, quality_cols), reverse=True)
    later_sum = jnp.concatenate([behind[0][1:], zero_row[None, :]], axis=0)
    later_norm = jnp.concatenate([behind[1][1:], zero_row[None, :]], axis=0)
    activity = (ahead[0] + later_sum) / jnp.sqrt(ahead[1] + later_norm)
    activity_t = activity.T
    activity_low = activity_t.astype(jnp.bfloat16)
    low_blocks = activity_low.reshape(FACTORS, blocks, FRAMES_DEV).transpose(1, 0, 2)

    def rebuild(triple):
        warped = warp_block(triple[0], triple[1])
        rebuilt = jnp.dot(triple[2].T, footprints, preferred_element_type=jnp.float32)
        return (warped.astype(jnp.float32) - rebuilt).astype(jnp.bfloat16)
    residual = lax.map(rebuild, (movie_blocks, shift_blocks, low_blocks)).reshape(FRAMES, ROWS * COLUMNS)
    return (activity_t, residual)
```

```python
import functools

import jax
import jax.numpy as jnp
from jax import lax
from jax.experimental import pallas as pl
from jax.experimental.pallas import tpu as pltpu
from jax.sharding import PartitionSpec as P

MESH = pl.DeviceIdType.MESH
HI = lax.Precision.HIGHEST
F32 = jnp.float32
BF16 = jnp.bfloat16


def lane_shift(x, d, fill):
    n = x.shape[1]
    lane = lax.broadcasted_iota(jnp.int32, x.shape, 1)
    keep = lane >= d if d > 0 else lane < n + d
    return jnp.where(keep, pltpu.roll(x, d % n, 1), fill)


def row_shift(x, d, fill):
    n = x.shape[0]
    row = lax.broadcasted_iota(jnp.int32, x.shape, 0)
    keep = row >= d if d > 0 else row < n + d
    return jnp.where(keep, pltpu.roll(x, d % n, 0), fill)


def row_turn(x, d):
    n = x.shape[0]
    d = d % n
    if d % 8 == 0:
        return jnp.concatenate([x[n - d :], x[: n - d]], axis=0)
    return pltpu.roll(x, d, 0)


def kernel(
    tm_n, strip_n,
    movie_h, shifts_r, proj_h, foot_h, quality_r, cont_r, ret_r,
    act_h, res_h,
    movie_v, proj_v, foot_v, warp_v, halo_v, shift_v,
    col_v, rows_v, prefix_v, suffix_v, scale_v, coef_v, part_v,
    rs_v, all_v, tm_v, carry_v, out_v,
    load_sem, halo_send, halo_recv, rs_send, rs_recv, tm_send, tm_recv,
    ag_send, ag_recv, cs_send, cs_recv, out_sem,
):
    frames, pixels = movie_v.shape
    factors = proj_v.shape[1]
    rows = shifts_r.shape[0]
    cols = pixels // rows
    share = frames // strip_n
    steps = frames.bit_length() - 1
    me_t = lax.axis_index("tm")
    me_s = lax.axis_index("strip")
    halves = [slice(i, i + 128) for i in range(0, factors, 128)]

    chunks = 4
    wide = pixels // chunks
    loads = []
    for c in range(chunks):
        part = pl.ds(c * wide, wide)
        loads.append((
            pltpu.make_async_copy(movie_h.at[:, part], movie_v.at[:, part], load_sem.at[2 * c]),
            pltpu.make_async_copy(proj_h.at[part], proj_v.at[part], load_sem.at[2 * c + 1]),
        ))
    foot_load = pltpu.make_async_copy(foot_h, foot_v, load_sem.at[2 * chunks])
    for pair in loads:
        for copy in pair:
            copy.start()

    barrier = pltpu.get_barrier_semaphore()

    def hail_strip(d, _):
        pl.semaphore_signal(
            barrier, inc=1, device_id={"strip": lax.rem(me_s + d, strip_n)}, device_id_type=MESH
        )
        return 0

    def hail_tm(d, _):
        pl.semaphore_signal(
            barrier, inc=1, device_id={"tm": lax.rem(me_t + d, tm_n)}, device_id_type=MESH
        )
        return 0

    lax.fori_loop(1, strip_n, hail_strip, 0)
    lax.fori_loop(1, tm_n, hail_tm, 0)
    pl.semaphore_wait(barrier, strip_n - 1 + tm_n - 1)

    def halo_copy(side):
        source = pl.ds((rows - 1) * cols, cols) if side == 0 else pl.ds(0, cols)
        target = me_s + 1 if side == 0 else me_s - 1
        return pltpu.make_async_remote_copy(
            src_ref=movie_h.at[:, source], dst_ref=halo_v.at[side],
            send_sem=halo_send.at[side], recv_sem=halo_recv.at[side],
            device_id={"strip": target}, device_id_type=MESH,
        )

    @pl.when(me_s < strip_n - 1)
    def _():
        halo_copy(0).start()

    @pl.when(me_s > 0)
    def _():
        halo_copy(1).start()

    @pl.when(me_s == 0)
    def _():
        halo_v[0] = jnp.zeros((frames, cols), BF16)

    @pl.when(me_s == strip_n - 1)
    def _():
        halo_v[1] = jnp.zeros((frames, cols), BF16)

    shifts = jnp.concatenate([shifts_r[...], jnp.zeros((frames - rows, frames), F32)], axis=0).T
    for h in range(rows):
        shift_v[h] = jnp.broadcast_to(shifts[:, h : h + 1], (frames, 128))

    quality, cont = quality_r[...], cont_r[...]
    ret = ret_r[...]
    powers = [ret]
    for _ in range(steps):
        powers.append(powers[-1] * powers[-1])
    prefix, suffix = cont, cont
    for level in range(steps):
        d = 1 << level
        prefix = prefix * lane_shift(prefix, d, 1.0)
        suffix = suffix * lane_shift(suffix, -d, 1.0)
    after = lane_shift(suffix, -1, 1.0)
    rows_v[0] = quality
    rows_v[1] = cont
    rows_v[2] = prefix
    rows_v[3] = after
    mine = [rows_v[i, pl.ds(me_t, 1), :] for i in range(4)]
    lane = lax.broadcasted_iota(jnp.int32, (1, frames), 1)
    ahead, behind = mine[1], mine[1]
    ahead_rows, behind_rows = [], []
    for level in range(steps):
        d = 1 << level
        ahead_rows.append(jnp.where(lane >= d, ahead, 0.0))
        behind_rows.append(jnp.where(lane < frames - d, behind, 0.0))
        ahead = ahead * lane_shift(ahead, d, 1.0)
        behind = behind * lane_shift(behind, -d, 1.0)
    lines = ahead_rows + behind_rows + mine
    lines = jnp.concatenate(lines + [jnp.zeros((frames - len(lines), frames), F32)], axis=0)
    turned = lines.T
    for i in range(2 * steps + 4):
        col_v[i] = jnp.broadcast_to(turned[:, i : i + 1], (frames, 128))
    QUALITY, CONT, PREFIX, AFTER = (2 * steps + i for i in range(4))

    small = [jnp.ones_like(ret), ret, powers[1], powers[1] * ret, powers[2]]
    small += [powers[2] * small[i] for i in (1, 2, 3)]
    rising = jnp.concatenate(small[1:] + [powers[3]], axis=0)
    falling = jnp.concatenate(small[::-1], axis=0)
    for level in range(3, steps):
        rising = jnp.concatenate([rising, rising * powers[level]], axis=0)
        falling = jnp.concatenate([falling * powers[level], falling], axis=0)
    for h in halves:
        prefix_v[:, h] = col_v[PREFIX] * rising[:, h]
        suffix_v[:, h] = col_v[AFTER] * falling[:, h]

    whole = prefix[:, frames - 1 : frames] * powers[steps]
    block = lax.broadcasted_iota(jnp.int32, (tm_n, factors), 0)
    before = jnp.where(block < me_t, whole, 1.0)
    beyond = jnp.where(block > me_t, whole, 1.0)
    d = 1
    while d < tm_n:
        before = before * row_shift(before, -d, 1.0)
        beyond = beyond * row_shift(beyond, d, 1.0)
        d *= 2
    before = jnp.where(block < me_t, row_shift(before, -1, 1.0), 0.0)
    beyond = jnp.where(block > me_t, row_shift(beyond, 1, 1.0), 0.0)
    for i, h in enumerate(halves):
        coef_v[i] = before[:, h]
        coef_v[len(halves) + i] = beyond[:, h]
    norm_in = jnp.sum(
        before * jnp.dot(quality * after, falling, precision=HI, preferred_element_type=F32),
        axis=0, keepdims=True,
    )
    norm_out = jnp.sum(
        beyond * jnp.dot(quality * prefix, rising, precision=HI, preferred_element_type=F32),
        axis=0, keepdims=True,
    )

    def smoothed(x, h):
        fore = x
        back = x * (col_v[CONT] * ret[:, h])
        for level in range(steps):
            d = 1 << level
            fore = fore + (col_v[level] * powers[level][:, h]) * row_turn(fore, d)
            back = back + (col_v[steps + level] * powers[level][:, h]) * row_turn(back, -d)
        row = lax.broadcasted_iota(jnp.int32, back.shape, 0)
        return fore + jnp.where(row < frames - 1, row_turn(back, -1), 0.0)

    for h in halves:
        norm = smoothed(col_v[QUALITY], h)
        norm = norm + prefix_v[:, h] * norm_in[:, h] + suffix_v[:, h] * norm_out[:, h]
        scale_v[:, h] = 1.0 / jnp.sqrt(norm)

    def warp_row(h, above, own, below):
        s = shift_v[h]
        near = jnp.abs(s)
        keep = jnp.maximum(0.0, 1.0 - near)
        down = s > 0.0
        for w in range(0, cols, 128):
            w = slice(w, w + 128)
            other = jnp.where(down, below[:, w].astype(F32), above[:, w].astype(F32))
            warped = keep * own[:, w].astype(F32) + near * other
            yield w, warped.astype(BF16)

    def row_ref(h):
        return movie_v.at[:, pl.ds(pl.multiple_of(h * cols, cols), cols)]

    def do_row(h, above, below):
        at = pl.multiple_of(h * cols, cols)
        for w, warped in warp_row(h, above[...], row_ref(h)[...], below[...]):
            warp_v[:, pl.ds(at + w.start, 128)] = warped
        part_v[...] += jnp.dot(
            warp_v[:, pl.ds(at, cols)], proj_v[pl.ds(at, cols), :], preferred_element_type=F32
        )

    part_v[...] = jnp.zeros((frames, factors), F32)
    done = 1
    for c in range(chunks):
        for copy in loads[c]:
            copy.wait()
        last = (c + 1) * rows // chunks - 1

        def inner(h, _):
            do_row(h, row_ref(h - 1), row_ref(h + 1))
            return 0

        lax.fori_loop(done, last, inner, 0)
        done = last
    foot_load.start()

    @pl.when(me_s > 0)
    def _():
        halo_copy(0).wait_recv()

    do_row(0, halo_v.at[0], row_ref(1))

    @pl.when(me_s < strip_n - 1)
    def _():
        halo_copy(1).wait_recv()

    do_row(rows - 1, row_ref(rows - 2), halo_v.at[1])

    def strip_peer(d):
        return lax.rem(me_s + d, strip_n)

    def rs_copy(peer):
        return pltpu.make_async_remote_copy(
            src_ref=part_v.at[pl.ds(pl.multiple_of(peer * share, share), share)],
            dst_ref=rs_v.at[me_s], send_sem=rs_send.at[peer], recv_sem=rs_recv.at[me_s],
            device_id={"strip": peer}, device_id_type=MESH,
        )

    def tm_copy(peer):
        return pltpu.make_async_remote_copy(
            src_ref=tm_v.at[me_t], dst_ref=tm_v.at[me_t],
            send_sem=tm_send.at[peer], recv_sem=tm_recv.at[me_t],
            device_id={"tm": peer}, device_id_type=MESH,
        )

    def ag_copy(peer):
        mine = pl.ds(pl.multiple_of(me_s * share, share), share)
        return pltpu.make_async_remote_copy(
            src_ref=all_v.at[mine], dst_ref=all_v.at[mine],
            send_sem=ag_send.at[peer], recv_sem=ag_recv.at[me_s],
            device_id={"strip": peer}, device_id_type=MESH,
        )

    def cs_copy(peer):
        return pltpu.make_async_remote_copy(
            src_ref=carry_v.at[me_s], dst_ref=carry_v.at[me_s],
            send_sem=cs_send.at[peer], recv_sem=cs_recv.at[me_s],
            device_id={"strip": peer}, device_id_type=MESH,
        )

    def each(count, start, make, act):
        def one(d, _):
            act(make(lax.rem(start + d, count)))
            return 0

        lax.fori_loop(1, count, one, 0)

    for i, h in enumerate(halves):
        weighted = part_v[:, h] * col_v[QUALITY]
        tm_v[me_t, i : i + 1] = jnp.sum(weighted * suffix_v[:, h], axis=0, keepdims=True)
        j = len(halves) + i
        tm_v[me_t, j : j + 1] = jnp.sum(weighted * prefix_v[:, h], axis=0, keepdims=True)
    each(strip_n, me_s, rs_copy, lambda copy: copy.start())
    each(tm_n, me_t, tm_copy, lambda copy: copy.start())

    def arrived(slot, ref, sem, **axis):
        pltpu.make_async_remote_copy(
            src_ref=ref, dst_ref=ref, send_sem=sem, recv_sem=sem,
            device_id=axis, device_id_type=MESH,
        ).wait_recv()

    rs_v[me_s] = part_v[pl.ds(pl.multiple_of(me_s * share, share), share), :]
    each(
        strip_n, me_s, lambda peer: peer,
        lambda peer: arrived(peer, rs_v.at[peer], rs_recv.at[peer], strip=peer),
    )
    total = rs_v[0]
    for i in range(1, strip_n):
        total = total + rs_v[i]
    all_v[pl.ds(pl.multiple_of(me_s * share, share), share), :] = total
    each(strip_n, me_s, ag_copy, lambda copy: copy.start())

    each(
        tm_n, me_t, lambda peer: peer,
        lambda peer: arrived(peer, tm_v.at[peer], tm_recv.at[peer], tm=peer),
    )
    for i in range(2 * len(halves)):
        carry_v[me_s, i : i + 1] = jnp.sum(coef_v[i] * tm_v[:, i, :], axis=0, keepdims=True)
    each(strip_n, me_s, cs_copy, lambda copy: copy.start())

    def share_of(peer):
        return all_v.at[pl.ds(pl.multiple_of(peer * share, share), share)]

    each(
        strip_n, me_s, lambda peer: peer,
        lambda peer: arrived(peer, share_of(peer), ag_recv.at[peer], strip=peer),
    )
    sums = []
    for h in halves:
        sums.append(smoothed(all_v[:, h] * col_v[QUALITY], h))
    each(
        strip_n, me_s, lambda peer: peer,
        lambda peer: arrived(peer, carry_v.at[peer], cs_recv.at[peer], strip=peer),
    )
    carried = carry_v[0]
    for i in range(1, strip_n):
        carried = carried + carry_v[i]
    low = []
    for i, h in enumerate(halves):
        j = len(halves) + i
        value = sums[i] + prefix_v[:, h] * carried[i : i + 1] + suffix_v[:, h] * carried[j : j + 1]
        value = value * scale_v[:, h]
        out_v[h, :] = value.T
        low.append(value.astype(BF16))
    low = jnp.concatenate(low, axis=1)
    per = factors // strip_n
    act_copy = pltpu.make_async_copy(
        out_v.at[pl.ds(pl.multiple_of(me_s * per, per), per)], act_h, out_sem.at[chunks]
    )
    act_copy.start()

    foot_load.wait()
    writes = []
    for c in range(chunks):

        def subtract(n, _):
            at = pl.ds(pl.multiple_of(n * cols, cols), cols)
            rebuilt = jnp.dot(low, foot_v[:, at], preferred_element_type=F32)
            warp_v[:, at] = (warp_v[:, at].astype(F32) - rebuilt).astype(BF16)
            return 0

        lax.fori_loop(c * rows // chunks, (c + 1) * rows // chunks, subtract, 0)
        part = pl.ds(c * wide, wide)
        copy = pltpu.make_async_copy(warp_v.at[:, part], res_h.at[:, part], out_sem.at[c])
        copy.start()
        writes.append(copy)

    @pl.when(me_s < strip_n - 1)
    def _():
        halo_copy(0).wait_send()

    @pl.when(me_s > 0)
    def _():
        halo_copy(1).wait_send()

    each(strip_n, me_s, rs_copy, lambda copy: copy.wait_send())
    each(tm_n, me_t, tm_copy, lambda copy: copy.wait_send())
    each(strip_n, me_s, ag_copy, lambda copy: copy.wait_send())
    each(strip_n, me_s, cs_copy, lambda copy: copy.wait_send())
    act_copy.wait()
    for copy in writes:
        copy.wait()


def body(tm_n, strip_n, movie, shifts, projection, footprints, quality, continuity, retention):
    frames, pixels = movie.shape
    factors = projection.shape[1]
    rows = shifts.shape[1]
    cols = pixels // rows
    per = factors // strip_n
    share = frames // strip_n
    halves = factors // 128
    steps = frames.bit_length() - 1
    DMA = pltpu.SemaphoreType.DMA
    vmem = pl.BlockSpec(memory_space=pltpu.VMEM)
    hbm = pl.BlockSpec(memory_space=pl.ANY)
    return pl.pallas_call(
        functools.partial(kernel, tm_n, strip_n),
        out_shape=(
            jax.ShapeDtypeStruct((per, frames), F32),
            jax.ShapeDtypeStruct((frames, pixels), BF16),
        ),
        in_specs=[hbm, vmem, hbm, hbm, vmem, vmem, vmem],
        out_specs=(hbm, hbm),
        scratch_shapes=[
            pltpu.VMEM((frames, pixels), BF16),
            pltpu.VMEM((pixels, factors), BF16),
            pltpu.VMEM((factors, pixels), BF16),
            pltpu.VMEM((frames, pixels), BF16),
            pltpu.VMEM((2, frames, cols), BF16),
            pltpu.VMEM((rows, frames, 128), F32),
            pltpu.VMEM((2 * steps + 4, frames, 128), F32),
            pltpu.VMEM((4, tm_n, frames), F32),
            pltpu.VMEM((frames, factors), F32),
            pltpu.VMEM((frames, factors), F32),
            pltpu.VMEM((frames, factors), F32),
            pltpu.VMEM((2 * halves, tm_n, 128), F32),
            pltpu.VMEM((frames, factors), F32),
            pltpu.VMEM((strip_n, share, factors), F32),
            pltpu.VMEM((frames, factors), F32),
            pltpu.VMEM((tm_n, 2 * halves, 128), F32),
            pltpu.VMEM((strip_n, 2 * halves, 128), F32),
            pltpu.VMEM((factors, frames), F32),
            DMA((9,)), DMA((2,)), DMA((2,)),
            DMA((strip_n,)), DMA((strip_n,)), DMA((tm_n,)), DMA((tm_n,)),
            DMA((strip_n,)), DMA((strip_n,)), DMA((strip_n,)), DMA((strip_n,)),
            DMA((5,)),
        ],
        compiler_params=pltpu.CompilerParams(collective_id=0, has_side_effects=True),
    )(
        movie, shifts.T, projection, footprints,
        quality.reshape(tm_n, frames), continuity.reshape(tm_n, frames), retention.reshape(1, factors),
    )


def solution(mesh):
    return jax.shard_map(
        functools.partial(body, mesh.shape["tm"], mesh.shape["strip"]),
        mesh=mesh,
        in_specs=(
            P("tm", "strip"), P("tm", "strip"), P("strip", None), P(None, "strip"), P(), P(), P(),
        ),
        out_specs=(P("strip", "tm"), P("tm", "strip")),
        check_vma=False,
    )
```

```python
import functools

import jax
import jax.numpy as jnp
from jax import lax
from jax.experimental import pallas as pl
from jax.experimental.pallas import tpu as pltpu
from jax.sharding import PartitionSpec as P

MESH = pl.DeviceIdType.MESH
HI = lax.Precision.HIGHEST
F32 = jnp.float32
BF16 = jnp.bfloat16


def lane_shift(x, d, fill):
    n = x.shape[1]
    lane = lax.broadcasted_iota(jnp.int32, x.shape, 1)
    keep = lane >= d if d > 0 else lane < n + d
    return jnp.where(keep, pltpu.roll(x, d % n, 1), fill)


def row_shift(x, d, fill):
    n = x.shape[0]
    row = lax.broadcasted_iota(jnp.int32, x.shape, 0)
    keep = row >= d if d > 0 else row < n + d
    return jnp.where(keep, pltpu.roll(x, d % n, 0), fill)


def row_turn(x, d):
    n = x.shape[0]
    d = d % n
    if d % 8 == 0:
        return jnp.concatenate([x[n - d :], x[: n - d]], axis=0)
    return pltpu.roll(x, d, 0)


def kernel(
    tm_n, strip_n,
    movie_h, shifts_h, proj_h, foot_h, quality_h, cont_h, ret_h,
    low_v, warp_v, foot_v, act_v,
    movie_v, proj_v, halo_v, shift_v, shifts_r, quality_r, cont_r, ret_r,
    col_v, rows_v, prefix_v, suffix_v, scale_v, coef_v, part_v,
    rs_v, all_v, tm_v, carry_v, out_v,
    load_sem, halo_send, halo_recv, rs_send, rs_recv, tm_send, tm_recv,
    ag_send, ag_recv, cs_send, cs_recv,
):
    frames, pixels = movie_v.shape
    factors = proj_v.shape[1]
    rows = shifts_r.shape[0]
    cols = pixels // rows
    share = frames // strip_n
    steps = frames.bit_length() - 1
    me_t = lax.axis_index("tm")
    me_s = lax.axis_index("strip")
    halves = [slice(i, i + 128) for i in range(0, factors, 128)]

    barrier = pltpu.get_barrier_semaphore()

    def hail_strip(d, _):
        pl.semaphore_signal(
            barrier, inc=1, device_id={"strip": lax.rem(me_s + d, strip_n)}, device_id_type=MESH
        )
        return 0

    def hail_tm(d, _):
        pl.semaphore_signal(
            barrier, inc=1, device_id={"tm": lax.rem(me_t + d, tm_n)}, device_id_type=MESH
        )
        return 0

    lax.fori_loop(1, strip_n, hail_strip, 0)
    lax.fori_loop(1, tm_n, hail_tm, 0)

    small = [
        pltpu.make_async_copy(source, target, load_sem.at[i])
        for i, (source, target) in enumerate(
            ((shifts_h, shifts_r), (quality_h, quality_r), (cont_h, cont_r), (ret_h, ret_r))
        )
    ]
    large = [
        pltpu.make_async_copy(movie_h, movie_v, load_sem.at[4]),
        pltpu.make_async_copy(proj_h, proj_v, load_sem.at[5]),
    ]
    foot_load = pltpu.make_async_copy(foot_h, foot_v, load_sem.at[6])
    for copy in small + large:
        copy.start()
    pl.semaphore_wait(barrier, strip_n - 1 + tm_n - 1)

    def halo_copy(side):
        source = pl.ds((rows - 1) * cols, cols) if side == 0 else pl.ds(0, cols)
        target = me_s + 1 if side == 0 else me_s - 1
        return pltpu.make_async_remote_copy(
            src_ref=movie_h.at[:, source], dst_ref=halo_v.at[side],
            send_sem=halo_send.at[side], recv_sem=halo_recv.at[side],
            device_id={"strip": target}, device_id_type=MESH,
        )

    @pl.when(me_s < strip_n - 1)
    def _():
        halo_copy(0).start()

    @pl.when(me_s > 0)
    def _():
        halo_copy(1).start()

    @pl.when(me_s == 0)
    def _():
        halo_v[0] = jnp.zeros((frames, cols), BF16)

    @pl.when(me_s == strip_n - 1)
    def _():
        halo_v[1] = jnp.zeros((frames, cols), BF16)

    for copy in small:
        copy.wait()

    shifts = jnp.concatenate([shifts_r[...], jnp.zeros((frames - rows, frames), F32)], axis=0).T
    for h in range(rows):
        shift_v[h] = jnp.broadcast_to(shifts[:, h : h + 1], (frames, 128))

    quality, cont = quality_r[...], cont_r[...]
    ret = ret_r[...]
    powers = [ret]
    for _ in range(steps):
        powers.append(powers[-1] * powers[-1])
    prefix, suffix = cont, cont
    for level in range(steps):
        d = 1 << level
        prefix = prefix * lane_shift(prefix, d, 1.0)
        suffix = suffix * lane_shift(suffix, -d, 1.0)
    after = lane_shift(suffix, -1, 1.0)
    rows_v[0] = quality
    rows_v[1] = cont
    rows_v[2] = prefix
    rows_v[3] = after
    mine = [rows_v[i, pl.ds(me_t, 1), :] for i in range(4)]
    lane = lax.broadcasted_iota(jnp.int32, (1, frames), 1)
    ahead, behind = mine[1], mine[1]
    ahead_rows, behind_rows = [], []
    for level in range(steps):
        d = 1 << level
        ahead_rows.append(jnp.where(lane >= d, ahead, 0.0))
        behind_rows.append(jnp.where(lane < frames - d, behind, 0.0))
        ahead = ahead * lane_shift(ahead, d, 1.0)
        behind = behind * lane_shift(behind, -d, 1.0)
    lines = ahead_rows + behind_rows + mine
    lines = jnp.concatenate(lines + [jnp.zeros((frames - len(lines), frames), F32)], axis=0)
    turned = lines.T
    for i in range(2 * steps + 4):
        col_v[i] = jnp.broadcast_to(turned[:, i : i + 1], (frames, 128))
    QUALITY, CONT, PREFIX, AFTER = (2 * steps + i for i in range(4))

    small = [jnp.ones_like(ret), ret, powers[1], powers[1] * ret, powers[2]]
    small += [powers[2] * small[i] for i in (1, 2, 3)]
    rising = jnp.concatenate(small[1:] + [powers[3]], axis=0)
    falling = jnp.concatenate(small[::-1], axis=0)
    for level in range(3, steps):
        rising = jnp.concatenate([rising, rising * powers[level]], axis=0)
        falling = jnp.concatenate([falling * powers[level], falling], axis=0)
    for h in halves:
        prefix_v[:, h] = col_v[PREFIX] * rising[:, h]
        suffix_v[:, h] = col_v[AFTER] * falling[:, h]

    def warp_row(h, above, own, below):
        s = shift_v[h]
        near = jnp.abs(s)
        keep = jnp.maximum(0.0, 1.0 - near)
        down = s > 0.0
        for w in range(0, cols, 128):
            w = slice(w, w + 128)
            other = jnp.where(down, below[:, w].astype(F32), above[:, w].astype(F32))
            warped = keep * own[:, w].astype(F32) + near * other
            yield w, warped.astype(BF16)

    def row_ref(h):
        return movie_v.at[:, h * cols : (h + 1) * cols]

    def warp_into(h, above, below):
        for w, warped in warp_row(h, above[...], row_ref(h)[...], below[...]):
            warp_v[:, h * cols + w.start : h * cols + w.stop] = warped

    def project(first, last):
        at = slice(first * cols, last * cols)
        return jnp.dot(warp_v[:, at], proj_v[at, :], preferred_element_type=F32)

    for copy in large:
        copy.wait()
    group = 4
    for first in range(1, rows - 1, group):
        last = min(first + group, rows - 1)
        for h in range(first, last):
            warp_into(h, row_ref(h - 1), row_ref(h + 1))
        inner = project(first, last)
        part_v[...] = inner if first == 1 else part_v[...] + inner
    foot_load.start()

    @pl.when(me_s > 0)
    def _():
        halo_copy(0).wait_recv()

    warp_into(0, halo_v.at[0], row_ref(1))
    part_v[...] += project(0, 1)

    @pl.when(me_s < strip_n - 1)
    def _():
        halo_copy(1).wait_recv()

    warp_into(rows - 1, row_ref(rows - 2), halo_v.at[1])
    part_v[...] += project(rows - 1, rows)

    def strip_peer(d):
        return lax.rem(me_s + d, strip_n)

    def rs_copy(peer):
        return pltpu.make_async_remote_copy(
            src_ref=part_v.at[pl.ds(pl.multiple_of(peer * share, share), share)],
            dst_ref=rs_v.at[me_s], send_sem=rs_send.at[peer], recv_sem=rs_recv.at[me_s],
            device_id={"strip": peer}, device_id_type=MESH,
        )

    def tm_copy(peer):
        return pltpu.make_async_remote_copy(
            src_ref=tm_v.at[me_t], dst_ref=tm_v.at[me_t],
            send_sem=tm_send.at[peer], recv_sem=tm_recv.at[me_t],
            device_id={"tm": peer}, device_id_type=MESH,
        )

    def ag_copy(peer):
        mine = pl.ds(pl.multiple_of(me_s * share, share), share)
        return pltpu.make_async_remote_copy(
            src_ref=all_v.at[mine], dst_ref=all_v.at[mine],
            send_sem=ag_send.at[peer], recv_sem=ag_recv.at[me_s],
            device_id={"strip": peer}, device_id_type=MESH,
        )

    def cs_copy(peer):
        return pltpu.make_async_remote_copy(
            src_ref=carry_v.at[me_s], dst_ref=carry_v.at[me_s],
            send_sem=cs_send.at[peer], recv_sem=cs_recv.at[me_s],
            device_id={"strip": peer}, device_id_type=MESH,
        )

    def each(count, start, make, act):
        def one(d, _):
            act(make(lax.rem(start + d, count)))
            return 0

        lax.fori_loop(1, count, one, 0)

    for i, h in enumerate(halves):
        weighted = part_v[:, h] * col_v[QUALITY]
        tm_v[me_t, i : i + 1] = jnp.sum(weighted * suffix_v[:, h], axis=0, keepdims=True)
        j = len(halves) + i
        tm_v[me_t, j : j + 1] = jnp.sum(weighted * prefix_v[:, h], axis=0, keepdims=True)
    each(strip_n, me_s, rs_copy, lambda copy: copy.start())
    each(tm_n, me_t, tm_copy, lambda copy: copy.start())

    def arrived(slot, ref, sem, **axis):
        pltpu.make_async_remote_copy(
            src_ref=ref, dst_ref=ref, send_sem=sem, recv_sem=sem,
            device_id=axis, device_id_type=MESH,
        ).wait_recv()

    whole = prefix[:, frames - 1 : frames] * powers[steps]
    block = lax.broadcasted_iota(jnp.int32, (tm_n, factors), 0)
    before = jnp.where(block < me_t, whole, 1.0)
    beyond = jnp.where(block > me_t, whole, 1.0)
    d = 1
    while d < tm_n:
        before = before * row_shift(before, -d, 1.0)
        beyond = beyond * row_shift(beyond, d, 1.0)
        d *= 2
    before = jnp.where(block < me_t, row_shift(before, -1, 1.0), 0.0)
    beyond = jnp.where(block > me_t, row_shift(beyond, 1, 1.0), 0.0)
    for i, h in enumerate(halves):
        coef_v[i] = before[:, h]
        coef_v[len(halves) + i] = beyond[:, h]
    norm_in = jnp.sum(
        before * jnp.dot(quality * after, falling, precision=HI, preferred_element_type=F32),
        axis=0, keepdims=True,
    )
    norm_out = jnp.sum(
        beyond * jnp.dot(quality * prefix, rising, precision=HI, preferred_element_type=F32),
        axis=0, keepdims=True,
    )

    rs_v[me_s] = part_v[pl.ds(pl.multiple_of(me_s * share, share), share), :]
    each(
        strip_n, me_s, lambda peer: peer,
        lambda peer: arrived(peer, rs_v.at[peer], rs_recv.at[peer], strip=peer),
    )
    total = rs_v[0]
    for i in range(1, strip_n):
        total = total + rs_v[i]
    all_v[pl.ds(pl.multiple_of(me_s * share, share), share), :] = total
    each(strip_n, me_s, ag_copy, lambda copy: copy.start())

    def smoothed(x, h):
        fore = x
        back = x * (col_v[CONT] * ret[:, h])
        for level in range(steps):
            d = 1 << level
            fore = fore + (col_v[level] * powers[level][:, h]) * row_turn(fore, d)
            back = back + (col_v[steps + level] * powers[level][:, h]) * row_turn(back, -d)
        row = lax.broadcasted_iota(jnp.int32, back.shape, 0)
        return fore + jnp.where(row < frames - 1, row_turn(back, -1), 0.0)

    for h in halves:
        norm = smoothed(col_v[QUALITY], h)
        norm = norm + prefix_v[:, h] * norm_in[:, h] + suffix_v[:, h] * norm_out[:, h]
        scale_v[:, h] = 1.0 / jnp.sqrt(norm)

    each(
        tm_n, me_t, lambda peer: peer,
        lambda peer: arrived(peer, tm_v.at[peer], tm_recv.at[peer], tm=peer),
    )
    for i in range(2 * len(halves)):
        carry_v[me_s, i : i + 1] = jnp.sum(coef_v[i] * tm_v[:, i, :], axis=0, keepdims=True)
    each(strip_n, me_s, cs_copy, lambda copy: copy.start())

    def share_of(peer):
        return all_v.at[pl.ds(pl.multiple_of(peer * share, share), share)]

    each(
        strip_n, me_s, lambda peer: peer,
        lambda peer: arrived(peer, share_of(peer), ag_recv.at[peer], strip=peer),
    )
    sums = []
    for h in halves:
        sums.append(smoothed(all_v[:, h] * col_v[QUALITY], h))
    each(
        strip_n, me_s, lambda peer: peer,
        lambda peer: arrived(peer, carry_v.at[peer], cs_recv.at[peer], strip=peer),
    )
    carried = carry_v[0]
    for i in range(1, strip_n):
        carried = carried + carry_v[i]
    for i, h in enumerate(halves):
        j = len(halves) + i
        value = sums[i] + prefix_v[:, h] * carried[i : i + 1] + suffix_v[:, h] * carried[j : j + 1]
        value = value * scale_v[:, h]
        out_v[h, :] = value.T
        low_v[:, h] = value.astype(BF16)
    per = factors // strip_n
    act_v[...] = out_v[pl.ds(pl.multiple_of(me_s * per, per), per), :]

    @pl.when(me_s < strip_n - 1)
    def _():
        halo_copy(0).wait_send()

    @pl.when(me_s > 0)
    def _():
        halo_copy(1).wait_send()

    each(strip_n, me_s, rs_copy, lambda copy: copy.wait_send())
    each(tm_n, me_t, tm_copy, lambda copy: copy.wait_send())
    each(strip_n, me_s, ag_copy, lambda copy: copy.wait_send())
    each(strip_n, me_s, cs_copy, lambda copy: copy.wait_send())
    foot_load.wait()


def rebuild(low_v, warp_v, foot_v, act_v, act_h, res_h, res_v, sem):
    pixels = warp_v.shape[1]
    tile, wide = 512, 1024
    copies = [pltpu.make_async_copy(act_v, act_h, sem.at[0])]
    copies[0].start()
    low = low_v[...]
    for at in range(0, pixels, wide):
        for n in range(at, at + wide, tile):
            n = slice(n, n + tile)
            rebuilt = jnp.dot(low, foot_v[:, n], preferred_element_type=F32)
            res_v[:, n] = (warp_v[:, n].astype(F32) - rebuilt).astype(BF16)
        part = pl.ds(at, wide)
        copy = pltpu.make_async_copy(res_v.at[:, part], res_h.at[:, part], sem.at[1 + at // wide])
        copy.start()
        copies.append(copy)
    for copy in copies:
        copy.wait()


def body(tm_n, strip_n, movie, shifts, projection, footprints, quality, continuity, retention):
    frames, pixels = movie.shape
    factors = projection.shape[1]
    rows = shifts.shape[1]
    cols = pixels // rows
    per = factors // strip_n
    share = frames // strip_n
    halves = factors // 128
    steps = frames.bit_length() - 1
    DMA = pltpu.SemaphoreType.DMA
    vmem = pl.BlockSpec(memory_space=pltpu.VMEM)
    hbm = pl.BlockSpec(memory_space=pltpu.HBM)
    low, warped, foot, act = pl.pallas_call(
        functools.partial(kernel, tm_n, strip_n),
        out_shape=(
            pltpu.VMEM((frames, factors), BF16),
            pltpu.VMEM((frames, pixels), BF16),
            pltpu.VMEM((factors, pixels), BF16),
            pltpu.VMEM((per, frames), F32),
        ),
        in_specs=[hbm] * 7,
        out_specs=(vmem,) * 4,
        scratch_shapes=[
            pltpu.VMEM((frames, pixels), BF16),
            pltpu.VMEM((pixels, factors), BF16),
            pltpu.VMEM((2, frames, cols), BF16),
            pltpu.VMEM((rows, frames, 128), F32),
            pltpu.VMEM((rows, frames), F32),
            pltpu.VMEM((tm_n, frames), F32),
            pltpu.VMEM((tm_n, frames), F32),
            pltpu.VMEM((1, factors), F32),
            pltpu.VMEM((2 * steps + 4, frames, 128), F32),
            pltpu.VMEM((4, tm_n, frames), F32),
            pltpu.VMEM((frames, factors), F32),
            pltpu.VMEM((frames, factors), F32),
            pltpu.VMEM((frames, factors), F32),
            pltpu.VMEM((2 * halves, tm_n, 128), F32),
            pltpu.VMEM((frames, factors), F32),
            pltpu.VMEM((strip_n, share, factors), F32),
            pltpu.VMEM((frames, factors), F32),
            pltpu.VMEM((tm_n, 2 * halves, 128), F32),
            pltpu.VMEM((strip_n, 2 * halves, 128), F32),
            pltpu.VMEM((factors, frames), F32),
            DMA((7,)), DMA((2,)), DMA((2,)),
            DMA((strip_n,)), DMA((strip_n,)), DMA((tm_n,)), DMA((tm_n,)),
            DMA((strip_n,)), DMA((strip_n,)), DMA((strip_n,)), DMA((strip_n,)),
        ],
        compiler_params=pltpu.CompilerParams(
            collective_id=0, has_side_effects=True, vmem_limit_bytes=32 << 20
        ),
    )(
        *(
            pltpu.with_memory_space_constraint(x, pltpu.HBM)
            for x in (
                movie, shifts.T, projection, footprints,
                quality.reshape(tm_n, frames), continuity.reshape(tm_n, frames),
                retention.reshape(1, factors),
            )
        )
    )
    return pl.pallas_call(
        rebuild,
        out_shape=(
            jax.ShapeDtypeStruct((per, frames), F32),
            jax.ShapeDtypeStruct((frames, pixels), BF16),
        ),
        in_specs=[vmem] * 4,
        out_specs=(hbm, hbm),
        scratch_shapes=[pltpu.VMEM((frames, pixels), BF16), DMA((1 + pixels // 1024,))],
        compiler_params=pltpu.CompilerParams(vmem_limit_bytes=16 << 20),
    )(low, warped, foot, act)


def solution(mesh):
    return jax.shard_map(
        functools.partial(body, mesh.shape["tm"], mesh.shape["strip"]),
        mesh=mesh,
        in_specs=(
            P("tm", "strip"), P("tm", "strip"), P("strip", None), P(None, "strip"), P(), P(), P(),
        ),
        out_specs=(P("strip", "tm"), P("tm", "strip")),
        check_vma=False,
    )
```

```python
import functools

import jax
import jax.numpy as jnp
from jax import lax
from jax.experimental import pallas as pl
from jax.experimental.pallas import tpu as pltpu
from jax.sharding import PartitionSpec as P

MESH = pl.DeviceIdType.MESH
HI = lax.Precision.HIGHEST
F32 = jnp.float32
BF16 = jnp.bfloat16
Z, CORES, Y = 8, 2, 4
ROUNDS = 4


def lane_shift(x, d, fill):
    n = x.shape[1]
    lane = lax.broadcasted_iota(jnp.int32, x.shape, 1)
    keep = lane >= d if d > 0 else lane < n + d
    return jnp.where(keep, pltpu.roll(x, d % n, 1), fill)


def row_shift(x, d, fill):
    n = x.shape[0]
    row = lax.broadcasted_iota(jnp.int32, x.shape, 0)
    keep = row >= d if d > 0 else row < n + d
    return jnp.where(keep, pltpu.roll(x, d % n, 0), fill)


def row_turn(x, d):
    n = x.shape[0]
    d = d % n
    if d % 8 == 0:
        return jnp.concatenate([x[n - d :], x[: n - d]], axis=0)
    return pltpu.roll(x, d, 0)


def kernel(
    tm_n, strip_n,
    movie_h, shifts_h, proj_h, foot_h, quality_h, cont_h, ret_h,
    low_v, warp_v, foot_v, act_v,
    movie_v, proj_v, halo_v, shift_v, shifts_r, quality_r, cont_r, ret_r,
    col_v, rows_v, prefix_v, suffix_v, scale_v, coef_v, part_v,
    rs_v, all_v, tm_v, carry_v, out_v,
    load_sem, halo_send, halo_recv, rs_send, rs_recv, tm_send, tm_recv,
    ag_send, ag_recv, cs_send, cs_recv, ends_v, sent_v, round_sem,
):
    frames, pixels = movie_v.shape
    factors = proj_v.shape[1]
    rows = shifts_r.shape[0]
    cols = pixels // rows
    share = frames // strip_n
    steps = frames.bit_length() - 1
    me_t = lax.axis_index("tm")
    me_s = lax.axis_index("strip")
    halves = [slice(i, i + 128) for i in range(0, factors, 128)]

    barrier = pltpu.get_barrier_semaphore()
    plane = Z * CORES
    other_x = lax.rem(me_t + plane, 2 * plane)
    flip = 1 - 2 * lax.rem(me_t, CORES)
    corner = me_s // Y * Y
    near = [
        {"tm": other_x},
        {"tm": other_x, "strip": lax.rem(me_s + Y, 2 * Y)},
        {"strip": corner + lax.rem(me_s + 1, Y)},
        {"strip": corner + lax.rem(me_s + Y - 1, Y)},
        {"tm": me_t // plane * plane + lax.rem(me_t + CORES, plane)},
        {"tm": me_t // plane * plane + lax.rem(me_t + plane - CORES, plane)},
    ]
    pair = [{"tm": me_t + flip}, {"tm": other_x + flip}]

    def hail(sem, partners):
        for partner in partners:
            pl.semaphore_signal(sem, inc=1, device_id=partner, device_id_type=MESH)

    @pl.when(me_s == Y - 1)
    def _():
        hail(barrier, [{"strip": Y}])

    @pl.when(me_s == Y)
    def _():
        hail(barrier, [{"strip": Y - 1}])

    hail(barrier, near + pair)

    def next_round(n):
        if n:
            pl.semaphore_wait(round_sem.at[n - 1], len(near))
        if n < ROUNDS:
            hail(round_sem.at[n], near)

    small = [
        pltpu.make_async_copy(source, target, load_sem.at[i])
        for i, (source, target) in enumerate(
            ((shifts_h, shifts_r), (quality_h, quality_r), (cont_h, cont_r), (ret_h, ret_r))
        )
    ]
    large = [
        pltpu.make_async_copy(movie_h, movie_v, load_sem.at[4]),
        pltpu.make_async_copy(proj_h, proj_v, load_sem.at[5]),
    ]
    foot_load = pltpu.make_async_copy(foot_h, foot_v, load_sem.at[6])
    for copy in small + large:
        copy.start()
    crossing = (me_s == Y - 1) | (me_s == Y)

    @pl.when(crossing)
    def _():
        pl.semaphore_wait(barrier, len(near) + len(pair) + 1)

    @pl.when(jnp.logical_not(crossing))
    def _():
        pl.semaphore_wait(barrier, len(near) + len(pair))

    def halo_copy(side):
        source = pl.ds((rows - 1) * cols, cols) if side == 0 else pl.ds(0, cols)
        target = me_s + 1 if side == 0 else me_s - 1
        return pltpu.make_async_remote_copy(
            src_ref=movie_h.at[:, source], dst_ref=halo_v.at[side],
            send_sem=halo_send.at[side], recv_sem=halo_recv.at[side],
            device_id={"strip": target}, device_id_type=MESH,
        )

    @pl.when(me_s < strip_n - 1)
    def _():
        halo_copy(0).start()

    @pl.when(me_s > 0)
    def _():
        halo_copy(1).start()

    @pl.when(me_s == 0)
    def _():
        halo_v[0] = jnp.zeros((frames, cols), BF16)

    @pl.when(me_s == strip_n - 1)
    def _():
        halo_v[1] = jnp.zeros((frames, cols), BF16)

    next_round(0)
    for copy in small:
        copy.wait()

    shifts = jnp.concatenate([shifts_r[...], jnp.zeros((frames - rows, frames), F32)], axis=0).T
    for h in range(rows):
        shift_v[h] = jnp.broadcast_to(shifts[:, h : h + 1], (frames, 128))

    quality, cont = quality_r[...], cont_r[...]
    ret = ret_r[...]
    powers = [ret]
    for _ in range(steps):
        powers.append(powers[-1] * powers[-1])
    prefix, suffix = cont, cont
    for level in range(steps):
        d = 1 << level
        prefix = prefix * lane_shift(prefix, d, 1.0)
        suffix = suffix * lane_shift(suffix, -d, 1.0)
    after = lane_shift(suffix, -1, 1.0)
    next_round(1)
    rows_v[0] = quality
    rows_v[1] = cont
    rows_v[2] = prefix
    rows_v[3] = after
    mine = [rows_v[i, pl.ds(me_t, 1), :] for i in range(4)]
    lane = lax.broadcasted_iota(jnp.int32, (1, frames), 1)
    ahead, behind = mine[1], mine[1]
    ahead_rows, behind_rows = [], []
    for level in range(steps):
        d = 1 << level
        ahead_rows.append(jnp.where(lane >= d, ahead, 0.0))
        behind_rows.append(jnp.where(lane < frames - d, behind, 0.0))
        ahead = ahead * lane_shift(ahead, d, 1.0)
        behind = behind * lane_shift(behind, -d, 1.0)
    lines = ahead_rows + behind_rows + mine
    lines = jnp.concatenate(lines + [jnp.zeros((frames - len(lines), frames), F32)], axis=0)
    turned = lines.T
    for i in range(2 * steps + 4):
        col_v[i] = jnp.broadcast_to(turned[:, i : i + 1], (frames, 128))
    QUALITY, CONT, PREFIX, AFTER = (2 * steps + i for i in range(4))

    small = [jnp.ones_like(ret), ret, powers[1], powers[1] * ret, powers[2]]
    small += [powers[2] * small[i] for i in (1, 2, 3)]
    rising = jnp.concatenate(small[1:] + [powers[3]], axis=0)
    falling = jnp.concatenate(small[::-1], axis=0)
    for level in range(3, steps):
        rising = jnp.concatenate([rising, rising * powers[level]], axis=0)
        falling = jnp.concatenate([falling * powers[level], falling], axis=0)
    for h in halves:
        prefix_v[:, h] = col_v[PREFIX] * rising[:, h]
        suffix_v[:, h] = col_v[AFTER] * falling[:, h]

    def warp_row(h, above, own, below):
        s = shift_v[h]
        near = jnp.abs(s)
        keep = jnp.maximum(0.0, 1.0 - near)
        down = s > 0.0
        for w in range(0, cols, 128):
            w = slice(w, w + 128)
            other = jnp.where(down, below[:, w].astype(F32), above[:, w].astype(F32))
            warped = keep * own[:, w].astype(F32) + near * other
            yield w, warped.astype(BF16)

    def row_ref(h):
        return movie_v.at[:, h * cols : (h + 1) * cols]

    def warp_into(h, above, below):
        for w, warped in warp_row(h, above[...], row_ref(h)[...], below[...]):
            warp_v[:, h * cols + w.start : h * cols + w.stop] = warped

    def project(first, last):
        at = slice(first * cols, last * cols)
        return jnp.dot(warp_v[:, at], proj_v[at, :], preferred_element_type=F32)

    next_round(2)
    for copy in large:
        copy.wait()
    group = 4
    for first in range(1, rows - 1, group):
        last = min(first + group, rows - 1)
        for h in range(first, last):
            warp_into(h, row_ref(h - 1), row_ref(h + 1))
        inner = project(first, last)
        part_v[...] = inner if first == 1 else part_v[...] + inner
        if first == 1 + 2 * group:
            next_round(3)
    foot_load.start()

    @pl.when(me_s > 0)
    def _():
        halo_copy(0).wait_recv()

    warp_into(0, halo_v.at[0], row_ref(1))
    part_v[...] += project(0, 1)

    @pl.when(me_s < strip_n - 1)
    def _():
        halo_copy(1).wait_recv()

    warp_into(rows - 1, row_ref(rows - 2), halo_v.at[1])
    part_v[...] += project(rows - 1, rows)

    def strip_peer(d):
        return lax.rem(me_s + d, strip_n)

    def rs_copy(peer):
        return pltpu.make_async_remote_copy(
            src_ref=sent_v.at[pl.ds(pl.multiple_of(peer * share, share), share)],
            dst_ref=rs_v.at[me_s], send_sem=rs_send.at[peer], recv_sem=rs_recv.at[me_s],
            device_id={"strip": peer}, device_id_type=MESH,
        )

    def tm_copy(d):
        peer = lax.rem(me_t + d, tm_n)
        return pltpu.make_async_remote_copy(
            src_ref=ends_v.at[(me_t + d) // tm_n], dst_ref=tm_v.at[me_t],
            send_sem=tm_send.at[peer], recv_sem=tm_recv.at[me_t],
            device_id={"tm": peer}, device_id_type=MESH,
        )

    def ag_copy(peer):
        mine = pl.ds(pl.multiple_of(me_s * share, share), share)
        return pltpu.make_async_remote_copy(
            src_ref=all_v.at[mine], dst_ref=all_v.at[mine],
            send_sem=ag_send.at[peer], recv_sem=ag_recv.at[me_s],
            device_id={"strip": peer}, device_id_type=MESH,
        )

    def cs_copy(peer):
        return pltpu.make_async_remote_copy(
            src_ref=carry_v.at[me_s], dst_ref=carry_v.at[me_s],
            send_sem=cs_send.at[peer], recv_sem=cs_recv.at[me_s],
            device_id={"strip": peer}, device_id_type=MESH,
        )

    def each_d(count, act):
        def one(d, _):
            act(d)
            return 0

        lax.fori_loop(1, count, one, 0)

    def each(count, start, make, act):
        def one(d, _):
            act(make(lax.rem(start + d, count)))
            return 0

        lax.fori_loop(1, count, one, 0)

    sent_v[...] = part_v[...].astype(BF16)
    for i, h in enumerate(halves):
        weighted = part_v[:, h] * col_v[QUALITY]
        ends_v[0, i : i + 1] = jnp.sum(weighted * suffix_v[:, h], axis=0, keepdims=True)
        ends_v[1, i : i + 1] = jnp.sum(weighted * prefix_v[:, h], axis=0, keepdims=True)
    tm_v[me_t] = jnp.zeros((len(halves), 128), F32)
    each(strip_n, me_s, rs_copy, lambda copy: copy.start())
    next_round(4)
    each_d(tm_n, lambda d: tm_copy(d).start())

    def arrived(slot, ref, sem, **axis):
        pltpu.make_async_remote_copy(
            src_ref=ref, dst_ref=ref, send_sem=sem, recv_sem=sem,
            device_id=axis, device_id_type=MESH,
        ).wait_recv()

    whole = prefix[:, frames - 1 : frames] * powers[steps]
    block = lax.broadcasted_iota(jnp.int32, (tm_n, factors), 0)
    before = jnp.where(block < me_t, whole, 1.0)
    beyond = jnp.where(block > me_t, whole, 1.0)
    d = 1
    while d < tm_n:
        before = before * row_shift(before, -d, 1.0)
        beyond = beyond * row_shift(beyond, d, 1.0)
        d *= 2
    before = jnp.where(block < me_t, row_shift(before, -1, 1.0), 0.0)
    beyond = jnp.where(block > me_t, row_shift(beyond, 1, 1.0), 0.0)
    for i, h in enumerate(halves):
        coef_v[i] = before[:, h]
        coef_v[len(halves) + i] = beyond[:, h]
    norm_in = jnp.sum(
        before * jnp.dot(quality * after, falling, precision=HI, preferred_element_type=F32),
        axis=0, keepdims=True,
    )
    norm_out = jnp.sum(
        beyond * jnp.dot(quality * prefix, rising, precision=HI, preferred_element_type=F32),
        axis=0, keepdims=True,
    )

    rs_v[me_s] = jnp.zeros((share, factors), BF16)
    each(
        strip_n, me_s, lambda peer: peer,
        lambda peer: arrived(peer, rs_v.at[peer], rs_recv.at[peer], strip=peer),
    )
    total = part_v[pl.ds(pl.multiple_of(me_s * share, share), share), :]
    for i in range(strip_n):
        total = total + rs_v[i].astype(F32)
    all_v[pl.ds(pl.multiple_of(me_s * share, share), share), :] = total.astype(BF16)
    each(strip_n, me_s, ag_copy, lambda copy: copy.start())

    def smoothed(x, h):
        fore = x
        back = x * (col_v[CONT] * ret[:, h])
        for level in range(steps):
            d = 1 << level
            fore = fore + (col_v[level] * powers[level][:, h]) * row_turn(fore, d)
            back = back + (col_v[steps + level] * powers[level][:, h]) * row_turn(back, -d)
        row = lax.broadcasted_iota(jnp.int32, back.shape, 0)
        return fore + jnp.where(row < frames - 1, row_turn(back, -1), 0.0)

    for h in halves:
        norm = smoothed(col_v[QUALITY], h)
        norm = norm + prefix_v[:, h] * norm_in[:, h] + suffix_v[:, h] * norm_out[:, h]
        scale_v[:, h] = 1.0 / jnp.sqrt(norm)

    each(
        tm_n, me_t, lambda peer: peer,
        lambda peer: arrived(peer, tm_v.at[peer], tm_recv.at[peer], tm=peer),
    )
    for i in range(len(halves)):
        for j in (i, len(halves) + i):
            carry_v[me_s, j : j + 1] = jnp.sum(coef_v[j] * tm_v[:, i, :], axis=0, keepdims=True)
    each(strip_n, me_s, cs_copy, lambda copy: copy.start())

    @pl.when(me_s < strip_n - 1)
    def _():
        halo_copy(0).wait_send()

    @pl.when(me_s > 0)
    def _():
        halo_copy(1).wait_send()

    each_d(tm_n, lambda d: tm_copy(d).wait_send())
    each(strip_n, me_s, rs_copy, lambda copy: copy.wait_send())

    def share_of(peer):
        return all_v.at[pl.ds(pl.multiple_of(peer * share, share), share)]

    each(
        strip_n, me_s, lambda peer: peer,
        lambda peer: arrived(peer, share_of(peer), ag_recv.at[peer], strip=peer),
    )
    sums = []
    for h in halves:
        sums.append(smoothed(all_v[:, h].astype(F32) * col_v[QUALITY], h))
    each(
        strip_n, me_s, lambda peer: peer,
        lambda peer: arrived(peer, carry_v.at[peer], cs_recv.at[peer], strip=peer),
    )
    carried = carry_v[0]
    for i in range(1, strip_n):
        carried = carried + carry_v[i]
    for i, h in enumerate(halves):
        j = len(halves) + i
        value = sums[i] + prefix_v[:, h] * carried[i : i + 1] + suffix_v[:, h] * carried[j : j + 1]
        value = value * scale_v[:, h]
        out_v[h, :] = value.T
        low_v[:, h] = value.astype(BF16)
    per = factors // strip_n
    act_v[...] = out_v[pl.ds(pl.multiple_of(me_s * per, per), per), :]

    each(strip_n, me_s, ag_copy, lambda copy: copy.wait_send())
    each(strip_n, me_s, cs_copy, lambda copy: copy.wait_send())
    foot_load.wait()


def rebuild(low_v, warp_v, foot_v, act_v, act_h, res_h, res_v, sem):
    pixels = warp_v.shape[1]
    tile, wide = 512, 1024
    copies = [pltpu.make_async_copy(act_v, act_h, sem.at[0])]
    copies[0].start()
    low = low_v[...]
    for at in range(0, pixels, wide):
        for n in range(at, at + wide, tile):
            n = slice(n, n + tile)
            rebuilt = jnp.dot(low, foot_v[:, n], preferred_element_type=F32)
            res_v[:, n] = (warp_v[:, n].astype(F32) - rebuilt).astype(BF16)
        part = pl.ds(at, wide)
        copy = pltpu.make_async_copy(res_v.at[:, part], res_h.at[:, part], sem.at[1 + at // wide])
        copy.start()
        copies.append(copy)
    for copy in copies:
        copy.wait()


def body(tm_n, strip_n, movie, shifts, projection, footprints, quality, continuity, retention):
    frames, pixels = movie.shape
    factors = projection.shape[1]
    rows = shifts.shape[1]
    cols = pixels // rows
    per = factors // strip_n
    share = frames // strip_n
    halves = factors // 128
    steps = frames.bit_length() - 1
    DMA = pltpu.SemaphoreType.DMA
    vmem = pl.BlockSpec(memory_space=pltpu.VMEM)
    hbm = pl.BlockSpec(memory_space=pltpu.HBM)
    low, warped, foot, act = pl.pallas_call(
        functools.partial(kernel, tm_n, strip_n),
        out_shape=(
            pltpu.VMEM((frames, factors), BF16),
            pltpu.VMEM((frames, pixels), BF16),
            pltpu.VMEM((factors, pixels), BF16),
            pltpu.VMEM((per, frames), F32),
        ),
        in_specs=[hbm] * 7,
        out_specs=(vmem,) * 4,
        scratch_shapes=[
            pltpu.VMEM((frames, pixels), BF16),
            pltpu.VMEM((pixels, factors), BF16),
            pltpu.VMEM((2, frames, cols), BF16),
            pltpu.VMEM((rows, frames, 128), F32),
            pltpu.VMEM((rows, frames), F32),
            pltpu.VMEM((tm_n, frames), F32),
            pltpu.VMEM((tm_n, frames), F32),
            pltpu.VMEM((1, factors), F32),
            pltpu.VMEM((2 * steps + 4, frames, 128), F32),
            pltpu.VMEM((4, tm_n, frames), F32),
            pltpu.VMEM((frames, factors), F32),
            pltpu.VMEM((frames, factors), F32),
            pltpu.VMEM((frames, factors), F32),
            pltpu.VMEM((2 * halves, tm_n, 128), F32),
            pltpu.VMEM((frames, factors), F32),
            pltpu.VMEM((strip_n, share, factors), BF16),
            pltpu.VMEM((frames, factors), BF16),
            pltpu.VMEM((tm_n, halves, 128), F32),
            pltpu.VMEM((strip_n, 2 * halves, 128), F32),
            pltpu.VMEM((factors, frames), F32),
            DMA((7,)), DMA((2,)), DMA((2,)),
            DMA((strip_n,)), DMA((strip_n,)), DMA((tm_n,)), DMA((tm_n,)),
            DMA((strip_n,)), DMA((strip_n,)), DMA((strip_n,)), DMA((strip_n,)),
            pltpu.VMEM((2, halves, 128), F32),
            pltpu.VMEM((frames, factors), BF16),
            pltpu.SemaphoreType.REGULAR((ROUNDS,)),
        ],
        compiler_params=pltpu.CompilerParams(
            collective_id=0, has_side_effects=True, vmem_limit_bytes=32 << 20
        ),
    )(
        *(
            pltpu.with_memory_space_constraint(x, pltpu.HBM)
            for x in (
                movie, shifts.T, projection, footprints,
                quality.reshape(tm_n, frames), continuity.reshape(tm_n, frames),
                retention.reshape(1, factors),
            )
        )
    )
    return pl.pallas_call(
        rebuild,
        out_shape=(
            jax.ShapeDtypeStruct((per, frames), F32),
            jax.ShapeDtypeStruct((frames, pixels), BF16),
        ),
        in_specs=[vmem] * 4,
        out_specs=(hbm, hbm),
        scratch_shapes=[pltpu.VMEM((frames, pixels), BF16), DMA((1 + pixels // 1024,))],
        compiler_params=pltpu.CompilerParams(vmem_limit_bytes=16 << 20),
    )(low, warped, foot, act)


def solution(mesh):
    return jax.shard_map(
        functools.partial(body, mesh.shape["tm"], mesh.shape["strip"]),
        mesh=mesh,
        in_specs=(
            P("tm", "strip"), P("tm", "strip"), P("strip", None), P(None, "strip"), P(), P(), P(),
        ),
        out_specs=(P("strip", "tm"), P("tm", "strip")),
        check_vma=False,
    )
```

```python
import functools

import jax
import jax.numpy as jnp
from jax import lax
from jax.experimental import pallas as pl
from jax.experimental.pallas import tpu as pltpu
from jax.sharding import PartitionSpec as P

MESH = pl.DeviceIdType.MESH
HI = lax.Precision.HIGHEST
F32 = jnp.float32
BF16 = jnp.bfloat16
Z, CORES, Y = 8, 2, 4
ROUNDS = 3


def lane_shift(x, d, fill):
    n = x.shape[1]
    lane = lax.broadcasted_iota(jnp.int32, x.shape, 1)
    keep = lane >= d if d > 0 else lane < n + d
    return jnp.where(keep, pltpu.roll(x, d % n, 1), fill)


def row_shift(x, d, fill):
    n = x.shape[0]
    row = lax.broadcasted_iota(jnp.int32, x.shape, 0)
    keep = row >= d if d > 0 else row < n + d
    return jnp.where(keep, pltpu.roll(x, d % n, 0), fill)


def row_turn(x, d):
    n = x.shape[0]
    d = d % n
    if d % 8 == 0:
        return jnp.concatenate([x[n - d :], x[: n - d]], axis=0)
    return pltpu.roll(x, d, 0)


def kernel(
    tm_n, strip_n,
    movie_h, shifts_h, proj_h, foot_h, quality_h, cont_h, ret_h,
    low_v, warp_v, foot_v, act_v,
    movie_v, proj_v, halo_v, shift_v, shifts_r, quality_r, cont_r, ret_r,
    col_v, rows_v, prefix_v, suffix_v, scale_v, coef_v, part_v,
    rs_v, all_v, tm_v, carry_v, out_v,
    load_sem, halo_send, halo_recv, sems, ends_v, sent_v, enter_v, table_v, round_sem,
):
    frames, pixels = movie_v.shape
    factors = proj_v.shape[1]
    rows = shifts_r.shape[0]
    cols = pixels // rows
    share = frames // strip_n
    steps = frames.bit_length() - 1
    me_t = lax.axis_index("tm")
    me_s = lax.axis_index("strip")
    halves = [slice(i, i + 128) for i in range(0, factors, 128)]

    barrier = pltpu.get_barrier_semaphore()
    plane = Z * CORES
    other_x = lax.rem(me_t + plane, 2 * plane)
    flip = 1 - 2 * lax.rem(me_t, CORES)
    corner = me_s // Y * Y
    planes = [me_t, other_x]
    place = lax.rem(me_t, plane)
    near = [
        {"tm": other_x},
        {"tm": other_x, "strip": lax.rem(me_s + Y, 2 * Y)},
        {"strip": corner + lax.rem(me_s + 1, Y)},
        {"strip": corner + lax.rem(me_s + Y - 1, Y)},
        {"tm": me_t // plane * plane + lax.rem(me_t + CORES, plane)},
        {"tm": me_t // plane * plane + lax.rem(me_t + plane - CORES, plane)},
    ]
    pair = [{"tm": me_t + flip}] + [{"tm": one["tm"] + flip} for one in near[4:]]

    def hail(sem, partners):
        for partner in partners:
            pl.semaphore_signal(sem, inc=1, device_id=partner, device_id_type=MESH)

    @pl.when(me_s == Y - 1)
    def _():
        hail(barrier, [{"strip": Y}])

    @pl.when(me_s == Y)
    def _():
        hail(barrier, [{"strip": Y - 1}])

    hail(barrier, near + pair)

    def next_round(n):
        if n:
            pl.semaphore_wait(round_sem.at[n - 1], len(near))
        if n < ROUNDS:
            hail(round_sem.at[n], near)

    small = [
        pltpu.make_async_copy(source, target, load_sem.at[i])
        for i, (source, target) in enumerate(
            ((shifts_h, shifts_r), (quality_h, quality_r), (cont_h, cont_r), (ret_h, ret_r))
        )
    ]
    large = [
        pltpu.make_async_copy(movie_h, movie_v, load_sem.at[4]),
        pltpu.make_async_copy(proj_h, proj_v, load_sem.at[5]),
    ]
    foot_load = pltpu.make_async_copy(foot_h, foot_v, load_sem.at[6])
    for copy in small + large:
        copy.start()
    crossing = (me_s == Y - 1) | (me_s == Y)

    @pl.when(crossing)
    def _():
        pl.semaphore_wait(barrier, len(near) + len(pair) + 1)

    @pl.when(jnp.logical_not(crossing))
    def _():
        pl.semaphore_wait(barrier, len(near) + len(pair))

    def halo_copy(side):
        source = pl.ds((rows - 1) * cols, cols) if side == 0 else pl.ds(0, cols)
        target = me_s + 1 if side == 0 else me_s - 1
        return pltpu.make_async_remote_copy(
            src_ref=movie_h.at[:, source], dst_ref=halo_v.at[side],
            send_sem=halo_send.at[side], recv_sem=halo_recv.at[side],
            device_id={"strip": target}, device_id_type=MESH,
        )

    @pl.when(me_s < strip_n - 1)
    def _():
        halo_copy(0).start()

    @pl.when(me_s > 0)
    def _():
        halo_copy(1).start()

    @pl.when(me_s == 0)
    def _():
        halo_v[0] = jnp.zeros((frames, cols), BF16)

    @pl.when(me_s == strip_n - 1)
    def _():
        halo_v[1] = jnp.zeros((frames, cols), BF16)

    next_round(0)
    for copy in small:
        copy.wait()

    shifts = jnp.concatenate([shifts_r[...], jnp.zeros((frames - rows, frames), F32)], axis=0).T
    for h in range(rows):
        shift_v[h] = jnp.broadcast_to(shifts[:, h : h + 1], (frames, 128))

    quality, cont = quality_r[...], cont_r[...]
    ret = ret_r[...]
    powers = [ret]
    for _ in range(steps):
        powers.append(powers[-1] * powers[-1])
    prefix, suffix = cont, cont
    for level in range(steps):
        d = 1 << level
        prefix = prefix * lane_shift(prefix, d, 1.0)
        suffix = suffix * lane_shift(suffix, -d, 1.0)
    after = lane_shift(suffix, -1, 1.0)
    next_round(1)
    rows_v[0] = quality
    rows_v[1] = cont
    rows_v[2] = prefix
    rows_v[3] = after
    mine = [rows_v[i, pl.ds(me_t, 1), :] for i in range(4)]
    lane = lax.broadcasted_iota(jnp.int32, (1, frames), 1)
    ahead, behind = mine[1], mine[1]
    ahead_rows, behind_rows = [], []
    for level in range(steps):
        d = 1 << level
        ahead_rows.append(jnp.where(lane >= d, ahead, 0.0))
        behind_rows.append(jnp.where(lane < frames - d, behind, 0.0))
        ahead = ahead * lane_shift(ahead, d, 1.0)
        behind = behind * lane_shift(behind, -d, 1.0)
    lines = ahead_rows + behind_rows + mine
    lines = jnp.concatenate(lines + [jnp.zeros((frames - len(lines), frames), F32)], axis=0)
    turned = lines.T
    for i in range(2 * steps + 4):
        col_v[i] = jnp.broadcast_to(turned[:, i : i + 1], (frames, 128))
    QUALITY, CONT, PREFIX, AFTER = (2 * steps + i for i in range(4))

    small = [jnp.ones_like(ret), ret, powers[1], powers[1] * ret, powers[2]]
    small += [powers[2] * small[i] for i in (1, 2, 3)]
    rising = jnp.concatenate(small[1:] + [powers[3]], axis=0)
    falling = jnp.concatenate(small[::-1], axis=0)
    for level in range(3, steps):
        rising = jnp.concatenate([rising, rising * powers[level]], axis=0)
        falling = jnp.concatenate([falling * powers[level], falling], axis=0)
    for h in halves:
        prefix_v[:, h] = col_v[PREFIX] * rising[:, h]
        suffix_v[:, h] = col_v[AFTER] * falling[:, h]

    def warp_row(h, above, own, below):
        s = shift_v[h]
        near = jnp.abs(s)
        keep = jnp.maximum(0.0, 1.0 - near)
        down = s > 0.0
        for w in range(0, cols, 128):
            w = slice(w, w + 128)
            other = jnp.where(down, below[:, w].astype(F32), above[:, w].astype(F32))
            warped = keep * own[:, w].astype(F32) + near * other
            yield w, warped.astype(BF16)

    def row_ref(h):
        return movie_v.at[:, h * cols : (h + 1) * cols]

    def warp_into(h, above, below):
        for w, warped in warp_row(h, above[...], row_ref(h)[...], below[...]):
            warp_v[:, h * cols + w.start : h * cols + w.stop] = warped

    def project(first, last):
        at = slice(first * cols, last * cols)
        return jnp.dot(warp_v[:, at], proj_v[at, :], preferred_element_type=F32)

    next_round(2)
    for copy in large:
        copy.wait()
    group = 4
    for first in range(1, rows - 1, group):
        last = min(first + group, rows - 1)
        for h in range(first, last):
            warp_into(h, row_ref(h - 1), row_ref(h + 1))
        inner = project(first, last)
        part_v[...] = inner if first == 1 else part_v[...] + inner
        if first == 1 + 2 * group:
            next_round(3)
    foot_load.start()

    @pl.when(me_s > 0)
    def _():
        halo_copy(0).wait_recv()

    warp_into(0, halo_v.at[0], row_ref(1))
    part_v[...] += project(0, 1)

    @pl.when(me_s < strip_n - 1)
    def _():
        halo_copy(1).wait_recv()

    warp_into(rows - 1, row_ref(rows - 2), halo_v.at[1])
    part_v[...] += project(rows - 1, rows)

    def strip_peer(d):
        return lax.rem(me_s + d, strip_n)

    def rs_copy(peer):
        return pltpu.make_async_remote_copy(
            src_ref=sent_v.at[pl.ds(pl.multiple_of(peer * share, share), share)],
            dst_ref=rs_v.at[me_s], send_sem=sems.at[0], recv_sem=sems.at[1],
            device_id={"strip": peer}, device_id_type=MESH,
        )

    def tm_copy(peer):
        return pltpu.make_async_remote_copy(
            src_ref=ends_v, dst_ref=tm_v.at[place], send_sem=sems.at[2], recv_sem=sems.at[3],
            device_id={"tm": me_t // plane * plane + peer}, device_id_type=MESH,
        )

    def ag_copy(peer):
        mine = pl.ds(pl.multiple_of(me_s * share, share), share)
        return pltpu.make_async_remote_copy(
            src_ref=all_v.at[mine], dst_ref=all_v.at[mine],
            send_sem=sems.at[4], recv_sem=sems.at[5],
            device_id={"strip": peer}, device_id_type=MESH,
        )

    def cs_copy(j, peer):
        slot = j * strip_n + me_s
        return pltpu.make_async_remote_copy(
            src_ref=enter_v.at[j], dst_ref=carry_v.at[slot],
            send_sem=sems.at[6], recv_sem=sems.at[7],
            device_id={"tm": planes[j], "strip": peer}, device_id_type=MESH,
        )

    def each_cs(act):
        for j in range(len(planes)):

            def one(d, _):
                act(j, lax.rem(me_s + d, strip_n))
                return 0

            lax.fori_loop(1 if j == 0 else 0, strip_n, one, 0)

    def each(count, start, make, act):
        def one(d, _):
            act(make(lax.rem(start + d, count)))
            return 0

        lax.fori_loop(1, count, one, 0)

    sent_v[...] = part_v[...].astype(BF16)
    for i, h in enumerate(halves):
        weighted = part_v[:, h] * col_v[QUALITY]
        j = len(halves) + i
        ends_v[i : i + 1] = jnp.sum(weighted * suffix_v[:, h], axis=0, keepdims=True)
        ends_v[j : j + 1] = jnp.sum(weighted * prefix_v[:, h], axis=0, keepdims=True)
    tm_v[place] = ends_v[...]
    each(strip_n, me_s, rs_copy, lambda copy: copy.start())
    each(plane, place, tm_copy, lambda copy: copy.start())

    def settled(ref, count, i):
        part = ref.at[pl.ds(0, count)]
        pltpu.make_async_copy(part, part, sems.at[i]).wait()

    whole = prefix[:, frames - 1 : frames] * powers[steps]
    block = lax.broadcasted_iota(jnp.int32, (tm_n, factors), 0)
    mine = pl.ds(pl.multiple_of(me_t // plane * plane, plane), plane)
    for j, target in enumerate(planes):
        before = jnp.where(block < target, whole, 1.0)
        beyond = jnp.where(block > target, whole, 1.0)
        d = 1
        while d < tm_n:
            before = before * row_shift(before, -d, 1.0)
            beyond = beyond * row_shift(beyond, d, 1.0)
            d *= 2
        before = jnp.where(block < target, row_shift(before, -1, 1.0), 0.0)
        beyond = jnp.where(block > target, row_shift(beyond, 1, 1.0), 0.0)
        for i, h in enumerate(halves):
            table_v[i] = before[:, h]
            table_v[len(halves) + i] = beyond[:, h]
        for i in range(2 * len(halves)):
            coef_v[j, i] = table_v[i, mine, :]
        if j == 0:
            norm_in = jnp.sum(
                before
                * jnp.dot(quality * after, falling, precision=HI, preferred_element_type=F32),
                axis=0, keepdims=True,
            )
            norm_out = jnp.sum(
                beyond
                * jnp.dot(quality * prefix, rising, precision=HI, preferred_element_type=F32),
                axis=0, keepdims=True,
            )

    rs_v[me_s] = jnp.zeros((share, factors), BF16)
    settled(rs_v, strip_n - 1, 1)
    total = part_v[pl.ds(pl.multiple_of(me_s * share, share), share), :]
    for i in range(strip_n):
        total = total + rs_v[i].astype(F32)
    all_v[pl.ds(pl.multiple_of(me_s * share, share), share), :] = total.astype(BF16)
    each(strip_n, me_s, ag_copy, lambda copy: copy.start())

    settled(tm_v, plane - 1, 3)
    for i in range(2 * len(halves)):
        ends = tm_v[:, i, :]
        for j in range(len(planes)):
            enter_v[j, i : i + 1] = jnp.sum(coef_v[j, i] * ends, axis=0, keepdims=True)
    carry_v[me_s] = enter_v[0]
    each_cs(lambda j, peer: cs_copy(j, peer).start())
    def smoothed(x, h):
        fore = x
        back = x * (col_v[CONT] * ret[:, h])
        for level in range(steps):
            d = 1 << level
            fore = fore + (col_v[level] * powers[level][:, h]) * row_turn(fore, d)
            back = back + (col_v[steps + level] * powers[level][:, h]) * row_turn(back, -d)
        row = lax.broadcasted_iota(jnp.int32, back.shape, 0)
        return fore + jnp.where(row < frames - 1, row_turn(back, -1), 0.0)

    for h in halves:
        norm = smoothed(col_v[QUALITY], h)
        norm = norm + prefix_v[:, h] * norm_in[:, h] + suffix_v[:, h] * norm_out[:, h]
        scale_v[:, h] = 1.0 / jnp.sqrt(norm)

    @pl.when(me_s < strip_n - 1)
    def _():
        halo_copy(0).wait_send()

    @pl.when(me_s > 0)
    def _():
        halo_copy(1).wait_send()

    settled(rs_v, strip_n - 1, 0)
    settled(tm_v, plane - 1, 2)
    settled(carry_v, len(planes) * strip_n - 1, 6)
    foot_load.wait()
    settled(all_v, (strip_n - 1) * share, 5)
    sums = []
    for h in halves:
        sums.append(smoothed(all_v[:, h].astype(F32) * col_v[QUALITY], h))
    settled(carry_v, len(planes) * strip_n - 1, 7)
    carried = carry_v[0]
    for i in range(1, len(planes) * strip_n):
        carried = carried + carry_v[i]
    for i, h in enumerate(halves):
        j = len(halves) + i
        value = sums[i] + prefix_v[:, h] * carried[i : i + 1] + suffix_v[:, h] * carried[j : j + 1]
        value = value * scale_v[:, h]
        out_v[h, :] = value.T
        low_v[:, h] = value.astype(BF16)
    per = factors // strip_n
    act_v[...] = out_v[pl.ds(pl.multiple_of(me_s * per, per), per), :]

    settled(all_v, (strip_n - 1) * share, 4)


def rebuild(low_v, warp_v, foot_v, act_v, act_h, res_h, res_v, sem):
    pixels = warp_v.shape[1]
    tile, wide = 512, 1024
    copies = [pltpu.make_async_copy(act_v, act_h, sem.at[0])]
    copies[0].start()
    low = low_v[...]
    for at in range(0, pixels, wide):
        for n in range(at, at + wide, tile):
            n = slice(n, n + tile)
            rebuilt = jnp.dot(low, foot_v[:, n], preferred_element_type=F32)
            res_v[:, n] = (warp_v[:, n].astype(F32) - rebuilt).astype(BF16)
        part = pl.ds(at, wide)
        copy = pltpu.make_async_copy(res_v.at[:, part], res_h.at[:, part], sem.at[1 + at // wide])
        copy.start()
        copies.append(copy)
    for copy in copies:
        copy.wait()


def body(tm_n, strip_n, movie, shifts, projection, footprints, quality, continuity, retention):
    frames, pixels = movie.shape
    factors = projection.shape[1]
    rows = shifts.shape[1]
    cols = pixels // rows
    per = factors // strip_n
    share = frames // strip_n
    halves = factors // 128
    steps = frames.bit_length() - 1
    DMA = pltpu.SemaphoreType.DMA
    vmem = pl.BlockSpec(memory_space=pltpu.VMEM)
    hbm = pl.BlockSpec(memory_space=pltpu.HBM)
    low, warped, foot, act = pl.pallas_call(
        functools.partial(kernel, tm_n, strip_n),
        out_shape=(
            pltpu.VMEM((frames, factors), BF16),
            pltpu.VMEM((frames, pixels), BF16),
            pltpu.VMEM((factors, pixels), BF16),
            pltpu.VMEM((per, frames), F32),
        ),
        in_specs=[hbm] * 7,
        out_specs=(vmem,) * 4,
        scratch_shapes=[
            pltpu.VMEM((frames, pixels), BF16),
            pltpu.VMEM((pixels, factors), BF16),
            pltpu.VMEM((2, frames, cols), BF16),
            pltpu.VMEM((rows, frames, 128), F32),
            pltpu.VMEM((rows, frames), F32),
            pltpu.VMEM((tm_n, frames), F32),
            pltpu.VMEM((tm_n, frames), F32),
            pltpu.VMEM((1, factors), F32),
            pltpu.VMEM((2 * steps + 4, frames, 128), F32),
            pltpu.VMEM((4, tm_n, frames), F32),
            pltpu.VMEM((frames, factors), F32),
            pltpu.VMEM((frames, factors), F32),
            pltpu.VMEM((frames, factors), F32),
            pltpu.VMEM((2, 2 * halves, Z * CORES, 128), F32),
            pltpu.VMEM((frames, factors), F32),
            pltpu.VMEM((strip_n, share, factors), BF16),
            pltpu.VMEM((frames, factors), BF16),
            pltpu.VMEM((Z * CORES, 2 * halves, 128), F32),
            pltpu.VMEM((2 * strip_n, 2 * halves, 128), F32),
            pltpu.VMEM((factors, frames), F32),
            DMA((7,)), DMA((2,)), DMA((2,)),
            DMA((8,)),
            pltpu.VMEM((2 * halves, 128), F32),
            pltpu.VMEM((frames, factors), BF16),
            pltpu.VMEM((2, 2 * halves, 128), F32),
            pltpu.VMEM((2 * halves, tm_n, 128), F32),
            pltpu.SemaphoreType.REGULAR((ROUNDS,)),
        ],
        compiler_params=pltpu.CompilerParams(
            collective_id=0, has_side_effects=True, vmem_limit_bytes=32 << 20
        ),
    )(
        *(
            pltpu.with_memory_space_constraint(x, pltpu.HBM)
            for x in (
                movie, shifts.T, projection, footprints,
                quality.reshape(tm_n, frames), continuity.reshape(tm_n, frames),
                retention.reshape(1, factors),
            )
        )
    )
    return pl.pallas_call(
        rebuild,
        out_shape=(
            jax.ShapeDtypeStruct((per, frames), F32),
            jax.ShapeDtypeStruct((frames, pixels), BF16),
        ),
        in_specs=[vmem] * 4,
        out_specs=(hbm, hbm),
        scratch_shapes=[pltpu.VMEM((frames, pixels), BF16), DMA((1 + pixels // 1024,))],
        compiler_params=pltpu.CompilerParams(vmem_limit_bytes=16 << 20),
    )(low, warped, foot, act)


def solution(mesh):
    return jax.shard_map(
        functools.partial(body, mesh.shape["tm"], mesh.shape["strip"]),
        mesh=mesh,
        in_specs=(
            P("tm", "strip"), P("tm", "strip"), P("strip", None), P(None, "strip"), P(), P(), P(),
        ),
        out_specs=(P("strip", "tm"), P("tm", "strip")),
        check_vma=False,
    )
```

```python
import functools

import jax
import jax.numpy as jnp
from jax import lax
from jax.experimental import pallas as pl
from jax.experimental.pallas import tpu as pltpu
from jax.sharding import PartitionSpec as P

MESH = pl.DeviceIdType.MESH
HI = lax.Precision.HIGHEST
F32 = jnp.float32
BF16 = jnp.bfloat16
Z, CORES, Y = 8, 2, 4
ROUNDS = 3


def lane_shift(x, d, fill):
    n = x.shape[1]
    lane = lax.broadcasted_iota(jnp.int32, x.shape, 1)
    keep = lane >= d if d > 0 else lane < n + d
    return jnp.where(keep, pltpu.roll(x, d % n, 1), fill)


def row_shift(x, d, fill):
    n = x.shape[0]
    row = lax.broadcasted_iota(jnp.int32, x.shape, 0)
    keep = row >= d if d > 0 else row < n + d
    return jnp.where(keep, pltpu.roll(x, d % n, 0), fill)


def row_turn(x, d):
    n = x.shape[0]
    d = d % n
    if d % 8 == 0:
        return jnp.concatenate([x[n - d :], x[: n - d]], axis=0)
    return pltpu.roll(x, d, 0)


def kernel(
    tm_n, strip_n,
    movie_h, shifts_h, proj_h, foot_h, quality_h, cont_h, ret_h,
    low_v, warp_v, foot_v, act_v,
    movie_v, proj_v, halo_v, shift_v, shifts_r, quality_r, cont_r, ret_r,
    col_v, rows_v, prefix_v, suffix_v, scale_v, coef_v, part_v,
    rs_v, all_v, tm_v, carry_v, out_v,
    load_sem, halo_send, halo_recv, sems, ends_v, sent_v, enter_v, table_v, round_sem,
):
    frames, pixels = movie_v.shape
    factors = proj_v.shape[1]
    rows = shifts_r.shape[0]
    cols = pixels // rows
    share = frames // strip_n
    steps = frames.bit_length() - 1
    me_t = lax.axis_index("tm")
    me_s = lax.axis_index("strip")
    halves = [slice(i, i + 128) for i in range(0, factors, 128)]

    barrier = pltpu.get_barrier_semaphore()
    plane = Z * CORES
    other_x = lax.rem(me_t + plane, 2 * plane)
    flip = 1 - 2 * lax.rem(me_t, CORES)
    corner = me_s // Y * Y
    planes = [me_t, other_x]
    place = lax.rem(me_t, plane)
    near = [
        {"tm": other_x},
        {"tm": other_x, "strip": lax.rem(me_s + Y, 2 * Y)},
        {"strip": corner + lax.rem(me_s + 1, Y)},
        {"strip": corner + lax.rem(me_s + Y - 1, Y)},
        {"tm": me_t // plane * plane + lax.rem(me_t + CORES, plane)},
        {"tm": me_t // plane * plane + lax.rem(me_t + plane - CORES, plane)},
    ]
    pair = [{"tm": me_t + flip}] + [{"tm": one["tm"] + flip} for one in near[4:]]

    def hail(sem, partners):
        for partner in partners:
            pl.semaphore_signal(sem, inc=1, device_id=partner, device_id_type=MESH)

    @pl.when(me_s == Y - 1)
    def _():
        hail(barrier, [{"strip": Y}])

    @pl.when(me_s == Y)
    def _():
        hail(barrier, [{"strip": Y - 1}])

    hail(barrier, near + pair)

    def next_round(n):
        if n:
            pl.semaphore_wait(round_sem.at[n - 1], len(near))
        if n < ROUNDS:
            hail(round_sem.at[n], near)

    small = [
        pltpu.make_async_copy(source, target, load_sem.at[i])
        for i, (source, target) in enumerate(
            ((shifts_h, shifts_r), (quality_h, quality_r), (cont_h, cont_r), (ret_h, ret_r))
        )
    ]
    large = [
        pltpu.make_async_copy(movie_h, movie_v, load_sem.at[4]),
        pltpu.make_async_copy(proj_h, proj_v, load_sem.at[5]),
    ]
    foot_load = pltpu.make_async_copy(foot_h, foot_v, load_sem.at[6])
    for copy in small + large:
        copy.start()
    crossing = (me_s == Y - 1) | (me_s == Y)

    @pl.when(crossing)
    def _():
        pl.semaphore_wait(barrier, len(near) + len(pair) + 1)

    @pl.when(jnp.logical_not(crossing))
    def _():
        pl.semaphore_wait(barrier, len(near) + len(pair))

    def halo_copy(side):
        source = pl.ds((rows - 1) * cols, cols) if side == 0 else pl.ds(0, cols)
        target = me_s + 1 if side == 0 else me_s - 1
        return pltpu.make_async_remote_copy(
            src_ref=movie_h.at[:, source], dst_ref=halo_v.at[side],
            send_sem=halo_send.at[side], recv_sem=halo_recv.at[side],
            device_id={"strip": target}, device_id_type=MESH,
        )

    @pl.when(me_s < strip_n - 1)
    def _():
        halo_copy(0).start()

    @pl.when(me_s > 0)
    def _():
        halo_copy(1).start()

    @pl.when(me_s == 0)
    def _():
        halo_v[0] = jnp.zeros((frames, cols), BF16)

    @pl.when(me_s == strip_n - 1)
    def _():
        halo_v[1] = jnp.zeros((frames, cols), BF16)

    next_round(0)
    for copy in small:
        copy.wait()

    shifts = jnp.concatenate([shifts_r[...], jnp.zeros((frames - rows, frames), F32)], axis=0).T
    for h in range(rows):
        shift_v[h] = jnp.broadcast_to(shifts[:, h : h + 1], (frames, 128))

    quality, cont = quality_r[...], cont_r[...]
    ret = ret_r[...]
    powers = [ret]
    for _ in range(steps):
        powers.append(powers[-1] * powers[-1])
    prefix, suffix = cont, cont
    for level in range(steps):
        d = 1 << level
        prefix = prefix * lane_shift(prefix, d, 1.0)
        suffix = suffix * lane_shift(suffix, -d, 1.0)
    after = lane_shift(suffix, -1, 1.0)
    next_round(1)
    rows_v[0] = quality
    rows_v[1] = cont
    rows_v[2] = prefix
    rows_v[3] = after
    mine = [rows_v[i, pl.ds(me_t, 1), :] for i in range(4)]
    lane = lax.broadcasted_iota(jnp.int32, (1, frames), 1)
    ahead, behind = mine[1], mine[1]
    ahead_rows, behind_rows = [], []
    for level in range(steps):
        d = 1 << level
        ahead_rows.append(jnp.where(lane >= d, ahead, 0.0))
        behind_rows.append(jnp.where(lane < frames - d, behind, 0.0))
        ahead = ahead * lane_shift(ahead, d, 1.0)
        behind = behind * lane_shift(behind, -d, 1.0)
    lines = ahead_rows + behind_rows + mine
    lines = jnp.concatenate(lines + [jnp.zeros((frames - len(lines), frames), F32)], axis=0)
    turned = lines.T
    for i in range(2 * steps + 4):
        col_v[i] = jnp.broadcast_to(turned[:, i : i + 1], (frames, 128))
    QUALITY, CONT, PREFIX, AFTER = (2 * steps + i for i in range(4))

    small = [jnp.ones_like(ret), ret, powers[1], powers[1] * ret, powers[2]]
    small += [powers[2] * small[i] for i in (1, 2, 3)]
    rising = jnp.concatenate(small[1:] + [powers[3]], axis=0)
    falling = jnp.concatenate(small[::-1], axis=0)
    for level in range(3, steps):
        rising = jnp.concatenate([rising, rising * powers[level]], axis=0)
        falling = jnp.concatenate([falling * powers[level], falling], axis=0)
    for h in halves:
        prefix_v[:, h] = col_v[PREFIX] * rising[:, h]
        suffix_v[:, h] = col_v[AFTER] * falling[:, h]

    def warp_row(h, above, own, below):
        s = shift_v[h]
        near = jnp.abs(s)
        keep = jnp.maximum(0.0, 1.0 - near)
        down = s > 0.0
        for w in range(0, cols, 128):
            w = slice(w, w + 128)
            other = jnp.where(down, below[:, w].astype(F32), above[:, w].astype(F32))
            warped = keep * own[:, w].astype(F32) + near * other
            yield w, warped.astype(BF16)

    def row_ref(h):
        return movie_v.at[:, h * cols : (h + 1) * cols]

    def warp_into(h, above, below):
        for w, warped in warp_row(h, above[...], row_ref(h)[...], below[...]):
            warp_v[:, h * cols + w.start : h * cols + w.stop] = warped

    def project(first, last):
        at = slice(first * cols, last * cols)
        return jnp.dot(warp_v[:, at], proj_v[at, :], preferred_element_type=F32)

    next_round(2)
    for copy in large:
        copy.wait()
    group = 4
    for first in range(1, rows - 1, group):
        last = min(first + group, rows - 1)
        for h in range(first, last):
            warp_into(h, row_ref(h - 1), row_ref(h + 1))
        inner = project(first, last)
        part_v[...] = inner if first == 1 else part_v[...] + inner
        if first == 1 + 2 * group:
            next_round(3)
    foot_load.start()

    swap = me_s // Y - me_s // (Y + 1)

    def edge(n, _):
        side = lax.rem(n + swap, 2)

        @pl.when(me_s + side * (strip_n - 1) - me_s * side * 2 > 0)
        def _():
            pltpu.make_async_copy(halo_v.at[side], halo_v.at[side], halo_recv.at[side]).wait()

        at = pl.multiple_of(side * (rows - 1) * cols, cols)
        inner = pl.multiple_of((1 + side * (rows - 3)) * cols, cols)
        s = shift_v[side * (rows - 1)]
        near_weight = jnp.abs(s)
        keep = jnp.maximum(0.0, 1.0 - near_weight)
        outside = s * (2 * side - 1).astype(F32) > 0.0
        for w in range(0, cols, 128):
            other = jnp.where(
                outside,
                halo_v[side, :, w : w + 128].astype(F32),
                movie_v[:, pl.ds(inner + w, 128)].astype(F32),
            )
            own = movie_v[:, pl.ds(at + w, 128)].astype(F32)
            warp_v[:, pl.ds(at + w, 128)] = (keep * own + near_weight * other).astype(BF16)
        part_v[...] += jnp.dot(
            warp_v[:, pl.ds(at, cols)], proj_v[pl.ds(at, cols), :], preferred_element_type=F32
        )
        return 0

    lax.fori_loop(0, 2, edge, 0)

    def strip_peer(d):
        return lax.rem(me_s + d, strip_n)

    def rs_copy(peer):
        return pltpu.make_async_remote_copy(
            src_ref=sent_v.at[pl.ds(pl.multiple_of(peer * share, share), share)],
            dst_ref=rs_v.at[me_s], send_sem=sems.at[0], recv_sem=sems.at[1],
            device_id={"strip": peer}, device_id_type=MESH,
        )

    def tm_copy(peer):
        return pltpu.make_async_remote_copy(
            src_ref=ends_v, dst_ref=tm_v.at[place], send_sem=sems.at[2], recv_sem=sems.at[3],
            device_id={"tm": me_t // plane * plane + peer}, device_id_type=MESH,
        )

    def ag_copy(peer):
        mine = pl.ds(pl.multiple_of(me_s * share, share), share)
        return pltpu.make_async_remote_copy(
            src_ref=all_v.at[mine], dst_ref=all_v.at[mine],
            send_sem=sems.at[4], recv_sem=sems.at[5],
            device_id={"strip": peer}, device_id_type=MESH,
        )

    def cs_copy(j, peer):
        slot = j * strip_n + me_s
        return pltpu.make_async_remote_copy(
            src_ref=enter_v.at[j], dst_ref=carry_v.at[slot],
            send_sem=sems.at[6], recv_sem=sems.at[7],
            device_id={"tm": planes[j], "strip": peer}, device_id_type=MESH,
        )

    for i, h in enumerate(halves):
        weighted = part_v[:, h] * col_v[QUALITY]
        j = len(halves) + i
        ends_v[i : i + 1] = jnp.sum(weighted * suffix_v[:, h], axis=0, keepdims=True)
        ends_v[j : j + 1] = jnp.sum(weighted * prefix_v[:, h], axis=0, keepdims=True)
    tm_v[place] = ends_v[...]
    for dz in (4, 3, 5, 2, 6, 1, 7, 0):
        for dc in (1, 0):
            if dz or dc:
                other = lax.rem(place // CORES + dz, Z) * CORES + lax.rem(place + dc, CORES)
                tm_copy(other).start()
    sent_v[...] = part_v[...].astype(BF16)
    peers = [
        lax.rem(me_s // Y + dx, 2) * Y + lax.rem(me_s + dy, Y)
        for dx, dy in ((1, 2), (1, 1), (1, 3), (0, 2), (1, 0), (0, 1), (0, 3))
    ]
    for peer in peers:
        rs_copy(peer).start()

    def settled(ref, count, i):
        part = ref.at[pl.ds(0, count)]
        pltpu.make_async_copy(part, part, sems.at[i]).wait()

    whole = prefix[:, frames - 1 : frames] * powers[steps]
    block = lax.broadcasted_iota(jnp.int32, (tm_n, factors), 0)
    mine = pl.ds(pl.multiple_of(me_t // plane * plane, plane), plane)
    for j, target in enumerate(planes):
        before = jnp.where(block < target, whole, 1.0)
        beyond = jnp.where(block > target, whole, 1.0)
        d = 1
        while d < tm_n:
            before = before * row_shift(before, -d, 1.0)
            beyond = beyond * row_shift(beyond, d, 1.0)
            d *= 2
        before = jnp.where(block < target, row_shift(before, -1, 1.0), 0.0)
        beyond = jnp.where(block > target, row_shift(beyond, 1, 1.0), 0.0)
        for i, h in enumerate(halves):
            table_v[i] = before[:, h]
            table_v[len(halves) + i] = beyond[:, h]
        for i in range(2 * len(halves)):
            coef_v[j, i] = table_v[i, mine, :]
        if j == 0:
            norm_in = jnp.sum(
                before
                * jnp.dot(quality * after, falling, precision=HI, preferred_element_type=F32),
                axis=0, keepdims=True,
            )
            norm_out = jnp.sum(
                beyond
                * jnp.dot(quality * prefix, rising, precision=HI, preferred_element_type=F32),
                axis=0, keepdims=True,
            )

    rs_v[me_s] = jnp.zeros((share, factors), BF16)
    settled(rs_v, strip_n - 1, 1)
    total = part_v[pl.ds(pl.multiple_of(me_s * share, share), share), :]
    for i in range(strip_n):
        total = total + rs_v[i].astype(F32)
    all_v[pl.ds(pl.multiple_of(me_s * share, share), share), :] = total.astype(BF16)
    for peer in peers:
        ag_copy(peer).start()

    settled(tm_v, plane - 1, 3)
    for i in range(2 * len(halves)):
        ends = tm_v[:, i, :]
        for j in range(len(planes)):
            enter_v[j, i : i + 1] = jnp.sum(coef_v[j, i] * ends, axis=0, keepdims=True)
    carry_v[me_s] = enter_v[0]
    for j in (1, 0):
        for peer in peers + [me_s] * j:
            cs_copy(j, peer).start()
    def smoothed(x, h):
        fore = x
        back = x * (col_v[CONT] * ret[:, h])
        for level in range(steps):
            d = 1 << level
            fore = fore + (col_v[level] * powers[level][:, h]) * row_turn(fore, d)
            back = back + (col_v[steps + level] * powers[level][:, h]) * row_turn(back, -d)
        row = lax.broadcasted_iota(jnp.int32, back.shape, 0)
        return fore + jnp.where(row < frames - 1, row_turn(back, -1), 0.0)

    for h in halves:
        norm = smoothed(col_v[QUALITY], h)
        norm = norm + prefix_v[:, h] * norm_in[:, h] + suffix_v[:, h] * norm_out[:, h]
        scale_v[:, h] = 1.0 / jnp.sqrt(norm)

    @pl.when(me_s < strip_n - 1)
    def _():
        halo_copy(0).wait_send()

    @pl.when(me_s > 0)
    def _():
        halo_copy(1).wait_send()

    settled(rs_v, strip_n - 1, 0)
    settled(tm_v, plane - 1, 2)
    settled(carry_v, len(planes) * strip_n - 1, 6)
    foot_load.wait()
    settled(all_v, (strip_n - 1) * share, 5)
    sums = []
    for h in halves:
        sums.append(smoothed(all_v[:, h].astype(F32) * col_v[QUALITY], h))
    settled(carry_v, len(planes) * strip_n - 1, 7)
    carried = carry_v[0]
    for i in range(1, len(planes) * strip_n):
        carried = carried + carry_v[i]
    for i, h in enumerate(halves):
        j = len(halves) + i
        value = sums[i] + prefix_v[:, h] * carried[i : i + 1] + suffix_v[:, h] * carried[j : j + 1]
        value = value * scale_v[:, h]
        out_v[h, :] = value.T
        low_v[:, h] = value.astype(BF16)
    per = factors // strip_n
    act_v[...] = out_v[pl.ds(pl.multiple_of(me_s * per, per), per), :]

    settled(all_v, (strip_n - 1) * share, 4)


def rebuild(low_v, warp_v, foot_v, act_v, act_h, res_h, res_v, sem):
    pixels = warp_v.shape[1]
    tile, wide = 512, 512
    copies = [pltpu.make_async_copy(act_v, act_h, sem.at[0])]
    copies[0].start()
    low = low_v[...]
    for at in range(0, pixels, wide):
        for n in range(at, at + wide, tile):
            n = slice(n, n + tile)
            rebuilt = jnp.dot(low, foot_v[:, n], preferred_element_type=F32)
            res_v[:, n] = (warp_v[:, n].astype(F32) - rebuilt).astype(BF16)
        part = pl.ds(at, wide)
        copy = pltpu.make_async_copy(res_v.at[:, part], res_h.at[:, part], sem.at[1 + at // wide])
        copy.start()
        copies.append(copy)
    for copy in copies:
        copy.wait()


def body(tm_n, strip_n, movie, shifts, projection, footprints, quality, continuity, retention):
    frames, pixels = movie.shape
    factors = projection.shape[1]
    rows = shifts.shape[1]
    cols = pixels // rows
    per = factors // strip_n
    share = frames // strip_n
    halves = factors // 128
    steps = frames.bit_length() - 1
    DMA = pltpu.SemaphoreType.DMA
    vmem = pl.BlockSpec(memory_space=pltpu.VMEM)
    hbm = pl.BlockSpec(memory_space=pltpu.HBM)
    low, warped, foot, act = pl.pallas_call(
        functools.partial(kernel, tm_n, strip_n),
        out_shape=(
            pltpu.VMEM((frames, factors), BF16),
            pltpu.VMEM((frames, pixels), BF16),
            pltpu.VMEM((factors, pixels), BF16),
            pltpu.VMEM((per, frames), F32),
        ),
        in_specs=[hbm] * 7,
        out_specs=(vmem,) * 4,
        scratch_shapes=[
            pltpu.VMEM((frames, pixels), BF16),
            pltpu.VMEM((pixels, factors), BF16),
            pltpu.VMEM((2, frames, cols), BF16),
            pltpu.VMEM((rows, frames, 128), F32),
            pltpu.VMEM((rows, frames), F32),
            pltpu.VMEM((tm_n, frames), F32),
            pltpu.VMEM((tm_n, frames), F32),
            pltpu.VMEM((1, factors), F32),
            pltpu.VMEM((2 * steps + 4, frames, 128), F32),
            pltpu.VMEM((4, tm_n, frames), F32),
            pltpu.VMEM((frames, factors), F32),
            pltpu.VMEM((frames, factors), F32),
            pltpu.VMEM((frames, factors), F32),
            pltpu.VMEM((2, 2 * halves, Z * CORES, 128), F32),
            pltpu.VMEM((frames, factors), F32),
            pltpu.VMEM((strip_n, share, factors), BF16),
            pltpu.VMEM((frames, factors), BF16),
            pltpu.VMEM((Z * CORES, 2 * halves, 128), F32),
            pltpu.VMEM((2 * strip_n, 2 * halves, 128), F32),
            pltpu.VMEM((factors, frames), F32),
            DMA((7,)), DMA((2,)), DMA((2,)),
            DMA((8,)),
            pltpu.VMEM((2 * halves, 128), F32),
            pltpu.VMEM((frames, factors), BF16),
            pltpu.VMEM((2, 2 * halves, 128), F32),
            pltpu.VMEM((2 * halves, tm_n, 128), F32),
            pltpu.SemaphoreType.REGULAR((ROUNDS,)),
        ],
        compiler_params=pltpu.CompilerParams(
            collective_id=0, has_side_effects=True, vmem_limit_bytes=32 << 20
        ),
    )(
        *(
            pltpu.with_memory_space_constraint(x, pltpu.HBM)
            for x in (
                movie, shifts.T, projection, footprints,
                quality.reshape(tm_n, frames), continuity.reshape(tm_n, frames),
                retention.reshape(1, factors),
            )
        )
    )
    return pl.pallas_call(
        rebuild,
        out_shape=(
            jax.ShapeDtypeStruct((per, frames), F32),
            jax.ShapeDtypeStruct((frames, pixels), BF16),
        ),
        in_specs=[vmem] * 4,
        out_specs=(hbm, hbm),
        scratch_shapes=[pltpu.VMEM((frames, pixels), BF16), DMA((1 + pixels // 512,))],
        compiler_params=pltpu.CompilerParams(vmem_limit_bytes=16 << 20),
    )(low, warped, foot, act)


def solution(mesh):
    return jax.shard_map(
        functools.partial(body, mesh.shape["tm"], mesh.shape["strip"]),
        mesh=mesh,
        in_specs=(
            P("tm", "strip"), P("tm", "strip"), P("strip", None), P(None, "strip"), P(), P(), P(),
        ),
        out_specs=(P("strip", "tm"), P("tm", "strip")),
        check_vma=False,
    )
```

```python
import functools

import jax
import jax.numpy as jnp
from jax import lax
from jax.experimental import pallas as pl
from jax.experimental.pallas import tpu as pltpu
from jax.sharding import PartitionSpec as P

MESH = pl.DeviceIdType.MESH
HI = lax.Precision.HIGHEST
F32 = jnp.float32
BF16 = jnp.bfloat16
Z, CORES, Y = 8, 2, 4
ROUNDS = 3


def lane_shift(x, d, fill):
    n = x.shape[1]
    lane = lax.broadcasted_iota(jnp.int32, x.shape, 1)
    keep = lane >= d if d > 0 else lane < n + d
    return jnp.where(keep, pltpu.roll(x, d % n, 1), fill)


def row_shift(x, d, fill):
    n = x.shape[0]
    row = lax.broadcasted_iota(jnp.int32, x.shape, 0)
    keep = row >= d if d > 0 else row < n + d
    return jnp.where(keep, pltpu.roll(x, d % n, 0), fill)


def row_turn(x, d):
    n = x.shape[0]
    d = d % n
    if d % 8 == 0:
        return jnp.concatenate([x[n - d :], x[: n - d]], axis=0)
    return pltpu.roll(x, d, 0)


def kernel(
    tm_n, strip_n,
    movie_h, shifts_h, proj_h, foot_h, quality_h, cont_h, ret_h,
    low_v, warp_v, foot_v, act_v,
    movie_v, proj_v, halo_v, shift_v, shifts_r, quality_r, cont_r, ret_r,
    col_v, rows_v, prefix_v, suffix_v, scale_v, coef_v, part_v,
    rs_v, all_v, tm_v, carry_v,
    load_sem, halo_send, halo_recv, sems, ends_v, sent_v, enter_v, table_v, round_sem,
):
    frames, pixels = movie_v.shape
    factors = proj_v.shape[1]
    rows = shifts_r.shape[0]
    cols = pixels // rows
    share = frames // strip_n
    steps = frames.bit_length() - 1
    me_t = lax.axis_index("tm")
    me_s = lax.axis_index("strip")
    halves = [slice(i, i + 128) for i in range(0, factors, 128)]

    barrier = pltpu.get_barrier_semaphore()
    plane = Z * CORES
    other_x = lax.rem(me_t + plane, 2 * plane)
    flip = 1 - 2 * lax.rem(me_t, CORES)
    corner = me_s // Y * Y
    planes = [me_t, other_x]
    place = lax.rem(me_t, plane)
    near = [
        {"tm": other_x},
        {"tm": other_x, "strip": lax.rem(me_s + Y, 2 * Y)},
        {"strip": corner + lax.rem(me_s + 1, Y)},
        {"strip": corner + lax.rem(me_s + Y - 1, Y)},
        {"tm": me_t // plane * plane + lax.rem(me_t + CORES, plane)},
        {"tm": me_t // plane * plane + lax.rem(me_t + plane - CORES, plane)},
    ]
    pair = [{"tm": me_t + flip}] + [{"tm": one["tm"] + flip} for one in near[4:]]

    def hail(sem, partners):
        for partner in partners:
            pl.semaphore_signal(sem, inc=1, device_id=partner, device_id_type=MESH)

    @pl.when(me_s == Y - 1)
    def _():
        hail(barrier, [{"strip": Y}])

    @pl.when(me_s == Y)
    def _():
        hail(barrier, [{"strip": Y - 1}])

    hail(barrier, near + pair)

    def next_round(n):
        if n:
            pl.semaphore_wait(round_sem.at[n - 1], len(near))
        if n < ROUNDS:
            hail(round_sem.at[n], near)

    small = [
        pltpu.make_async_copy(source, target, load_sem.at[i])
        for i, (source, target) in enumerate(
            ((shifts_h, shifts_r), (quality_h, quality_r), (cont_h, cont_r), (ret_h, ret_r))
        )
    ]
    top, bottom = pl.ds(0, cols), pl.ds((rows - 1) * cols, cols)
    middle = pl.ds(cols, (rows - 2) * cols)
    edges = [
        pltpu.make_async_copy(movie_h.at[:, part], movie_v.at[:, part], load_sem.at[i])
        for i, part in ((7, top), (8, bottom))
    ]
    large = [
        pltpu.make_async_copy(movie_h.at[:, middle], movie_v.at[:, middle], load_sem.at[4]),
        pltpu.make_async_copy(proj_h, proj_v, load_sem.at[5]),
    ]
    foot_load = pltpu.make_async_copy(foot_h, foot_v, load_sem.at[6])
    for copy in edges + small + large:
        copy.start()
    for copy in edges:
        copy.wait()
    crossing = (me_s == Y - 1) | (me_s == Y)

    @pl.when(crossing)
    def _():
        pl.semaphore_wait(barrier, len(near) + len(pair) + 1)

    @pl.when(jnp.logical_not(crossing))
    def _():
        pl.semaphore_wait(barrier, len(near) + len(pair))

    def halo_copy(side):
        source = bottom if side == 0 else top
        target = me_s + 1 if side == 0 else me_s - 1
        return pltpu.make_async_remote_copy(
            src_ref=movie_v.at[:, source], dst_ref=halo_v.at[side],
            send_sem=halo_send.at[side], recv_sem=halo_recv.at[side],
            device_id={"strip": target}, device_id_type=MESH,
        )

    @pl.when(me_s < strip_n - 1)
    def _():
        halo_copy(0).start()

    @pl.when(me_s > 0)
    def _():
        halo_copy(1).start()

    @pl.when(me_s == 0)
    def _():
        halo_v[0] = jnp.zeros((frames, cols), BF16)

    @pl.when(me_s == strip_n - 1)
    def _():
        halo_v[1] = jnp.zeros((frames, cols), BF16)

    next_round(0)
    for copy in small:
        copy.wait()

    shifts = jnp.concatenate([shifts_r[...], jnp.zeros((frames - rows, frames), F32)], axis=0).T
    for h in range(rows):
        shift_v[h] = jnp.broadcast_to(shifts[:, h : h + 1], (frames, 128))

    quality, cont = quality_r[...], cont_r[...]
    ret = ret_r[...]
    powers = [ret]
    for _ in range(steps):
        powers.append(powers[-1] * powers[-1])
    prefix, suffix = cont, cont
    for level in range(steps):
        d = 1 << level
        prefix = prefix * lane_shift(prefix, d, 1.0)
        suffix = suffix * lane_shift(suffix, -d, 1.0)
    after = lane_shift(suffix, -1, 1.0)
    next_round(1)
    rows_v[0] = quality
    rows_v[1] = cont
    rows_v[2] = prefix
    rows_v[3] = after
    mine = [rows_v[i, pl.ds(me_t, 1), :] for i in range(4)]
    lane = lax.broadcasted_iota(jnp.int32, (1, frames), 1)
    ahead, behind = mine[1], mine[1]
    ahead_rows, behind_rows = [], []
    for level in range(steps):
        d = 1 << level
        ahead_rows.append(jnp.where(lane >= d, ahead, 0.0))
        behind_rows.append(jnp.where(lane < frames - d, behind, 0.0))
        ahead = ahead * lane_shift(ahead, d, 1.0)
        behind = behind * lane_shift(behind, -d, 1.0)
    lines = ahead_rows + behind_rows + mine
    lines = jnp.concatenate(lines + [jnp.zeros((frames - len(lines), frames), F32)], axis=0)
    turned = lines.T
    for i in range(2 * steps + 4):
        col_v[i] = jnp.broadcast_to(turned[:, i : i + 1], (frames, 128))
    QUALITY, CONT, PREFIX, AFTER = (2 * steps + i for i in range(4))

    small = [jnp.ones_like(ret), ret, powers[1], powers[1] * ret, powers[2]]
    small += [powers[2] * small[i] for i in (1, 2, 3)]
    rising = jnp.concatenate(small[1:] + [powers[3]], axis=0)
    falling = jnp.concatenate(small[::-1], axis=0)
    for level in range(3, steps):
        rising = jnp.concatenate([rising, rising * powers[level]], axis=0)
        falling = jnp.concatenate([falling * powers[level], falling], axis=0)
    for h in halves:
        prefix_v[:, h] = col_v[PREFIX] * rising[:, h]
        suffix_v[:, h] = col_v[AFTER] * falling[:, h]

    def warp_row(h, above, own, below):
        s = shift_v[h]
        near = jnp.abs(s)
        keep = jnp.maximum(0.0, 1.0 - near)
        down = s > 0.0
        for w in range(0, cols, 128):
            w = slice(w, w + 128)
            other = jnp.where(down, below[:, w].astype(F32), above[:, w].astype(F32))
            warped = keep * own[:, w].astype(F32) + near * other
            yield w, warped.astype(BF16)

    def row_ref(h):
        return movie_v.at[:, h * cols : (h + 1) * cols]

    def warp_into(h, above, below):
        for w, warped in warp_row(h, above[...], row_ref(h)[...], below[...]):
            warp_v[:, h * cols + w.start : h * cols + w.stop] = warped

    def project(first, last):
        at = slice(first * cols, last * cols)
        return jnp.dot(warp_v[:, at], proj_v[at, :], preferred_element_type=F32)

    next_round(2)
    for copy in large:
        copy.wait()
    group = 4
    for first in range(1, rows - 1, group):
        last = min(first + group, rows - 1)
        for h in range(first, last):
            warp_into(h, row_ref(h - 1), row_ref(h + 1))
        inner = project(first, last)
        part_v[...] = inner if first == 1 else part_v[...] + inner
        if first == 1 + 2 * group:
            next_round(3)
    foot_load.start()

    swap = me_s // Y - me_s // (Y + 1)

    def edge(n, _):
        side = lax.rem(n + swap, 2)

        @pl.when(me_s + side * (strip_n - 1) - me_s * side * 2 > 0)
        def _():
            pltpu.make_async_copy(halo_v.at[side], halo_v.at[side], halo_recv.at[side]).wait()

        at = pl.multiple_of(side * (rows - 1) * cols, cols)
        inner = pl.multiple_of((1 + side * (rows - 3)) * cols, cols)
        s = shift_v[side * (rows - 1)]
        near_weight = jnp.abs(s)
        keep = jnp.maximum(0.0, 1.0 - near_weight)
        outside = s * (2 * side - 1).astype(F32) > 0.0
        for w in range(0, cols, 128):
            other = jnp.where(
                outside,
                halo_v[side, :, w : w + 128].astype(F32),
                movie_v[:, pl.ds(inner + w, 128)].astype(F32),
            )
            own = movie_v[:, pl.ds(at + w, 128)].astype(F32)
            warp_v[:, pl.ds(at + w, 128)] = (keep * own + near_weight * other).astype(BF16)
        part_v[...] += jnp.dot(
            warp_v[:, pl.ds(at, cols)], proj_v[pl.ds(at, cols), :], preferred_element_type=F32
        )
        return 0

    lax.fori_loop(0, 2, edge, 0)

    def strip_peer(d):
        return lax.rem(me_s + d, strip_n)

    def rs_copy(peer):
        return pltpu.make_async_remote_copy(
            src_ref=sent_v.at[pl.ds(pl.multiple_of(peer * share, share), share)],
            dst_ref=rs_v.at[me_s], send_sem=sems.at[0], recv_sem=sems.at[1],
            device_id={"strip": peer}, device_id_type=MESH,
        )

    def tm_copy(peer):
        return pltpu.make_async_remote_copy(
            src_ref=ends_v, dst_ref=tm_v.at[place], send_sem=sems.at[2], recv_sem=sems.at[3],
            device_id={"tm": me_t // plane * plane + peer}, device_id_type=MESH,
        )

    def ag_copy(peer):
        mine = pl.ds(pl.multiple_of(me_s * share, share), share)
        return pltpu.make_async_remote_copy(
            src_ref=all_v.at[mine], dst_ref=all_v.at[mine],
            send_sem=sems.at[4], recv_sem=sems.at[5],
            device_id={"strip": peer}, device_id_type=MESH,
        )

    def cs_copy(j, peer):
        slot = j * strip_n + me_s
        return pltpu.make_async_remote_copy(
            src_ref=enter_v.at[j], dst_ref=carry_v.at[slot],
            send_sem=sems.at[6], recv_sem=sems.at[7],
            device_id={"tm": planes[j], "strip": peer}, device_id_type=MESH,
        )

    for i, h in enumerate(halves):
        weighted = part_v[:, h] * col_v[QUALITY]
        j = len(halves) + i
        ends_v[i : i + 1] = jnp.sum(weighted * suffix_v[:, h], axis=0, keepdims=True)
        ends_v[j : j + 1] = jnp.sum(weighted * prefix_v[:, h], axis=0, keepdims=True)
    tm_v[place] = ends_v[...]
    here_z, here_c = lax.div(place, CORES), lax.rem(place, CORES)
    for dz in (4, 3, 5, 2, 6, 1, 7, 0):
        floor = lax.rem(here_z + dz, Z) * CORES
        for core in (1 - here_c, here_c)[: 2 if dz else 1]:
            tm_copy(floor + core).start()
    across = lax.rem(me_s + Y, 2 * Y)
    corners = [lax.div(one, Y) * Y for one in (me_s, across)]
    ys = [lax.rem(me_s + dy, Y) for dy in range(Y)]
    peers = [
        corners[dx] + ys[dy]
        for dx, dy in ((1, 2), (1, 1), (1, 3), (0, 2), (1, 0), (0, 1), (0, 3))
    ]
    sent_v[...] = part_v[...].astype(BF16)
    for peer in peers:
        rs_copy(peer).start()

    def settled(ref, count, i):
        part = ref.at[pl.ds(0, count)]
        pltpu.make_async_copy(part, part, sems.at[i]).wait()

    whole = prefix[:, frames - 1 : frames] * powers[steps]
    block = lax.broadcasted_iota(jnp.int32, (tm_n, factors), 0)
    mine = pl.ds(pl.multiple_of(me_t // plane * plane, plane), plane)
    for j, target in enumerate(planes):
        before = jnp.where(block < target, whole, 1.0)
        beyond = jnp.where(block > target, whole, 1.0)
        d = 1
        while d < tm_n:
            before = before * row_shift(before, -d, 1.0)
            beyond = beyond * row_shift(beyond, d, 1.0)
            d *= 2
        before = jnp.where(block < target, row_shift(before, -1, 1.0), 0.0)
        beyond = jnp.where(block > target, row_shift(beyond, 1, 1.0), 0.0)
        for i, h in enumerate(halves):
            table_v[i] = before[:, h]
            table_v[len(halves) + i] = beyond[:, h]
        for i in range(2 * len(halves)):
            coef_v[j, i] = table_v[i, mine, :]
        if j == 0:
            norm_in = jnp.sum(
                before
                * jnp.dot(quality * after, falling, precision=HI, preferred_element_type=F32),
                axis=0, keepdims=True,
            )
            norm_out = jnp.sum(
                beyond
                * jnp.dot(quality * prefix, rising, precision=HI, preferred_element_type=F32),
                axis=0, keepdims=True,
            )

    rs_v[me_s] = jnp.zeros((share, factors), BF16)
    settled(rs_v, strip_n - 1, 1)
    total = part_v[pl.ds(pl.multiple_of(me_s * share, share), share), :]
    for i in range(strip_n):
        total = total + rs_v[i].astype(F32)
    all_v[pl.ds(pl.multiple_of(me_s * share, share), share), :] = total.astype(BF16)
    for peer in peers:
        ag_copy(peer).start()

    settled(tm_v, plane - 1, 3)
    for i in range(2 * len(halves)):
        ends = tm_v[:, i, :]
        for j in range(len(planes)):
            enter_v[j, i : i + 1] = jnp.sum(coef_v[j, i] * ends, axis=0, keepdims=True)
    carry_v[me_s] = enter_v[0]
    for j in (1, 0):
        for peer in peers + [me_s] * j:
            cs_copy(j, peer).start()
    def smoothed(x, h):
        fore = x
        back = x * (col_v[CONT] * ret[:, h])
        for level in range(steps):
            d = 1 << level
            fore = fore + (col_v[level] * powers[level][:, h]) * row_turn(fore, d)
            back = back + (col_v[steps + level] * powers[level][:, h]) * row_turn(back, -d)
        row = lax.broadcasted_iota(jnp.int32, back.shape, 0)
        return fore + jnp.where(row < frames - 1, row_turn(back, -1), 0.0)

    for h in halves:
        norm = smoothed(col_v[QUALITY], h)
        norm = norm + prefix_v[:, h] * norm_in[:, h] + suffix_v[:, h] * norm_out[:, h]
        scale_v[:, h] = 1.0 / jnp.sqrt(norm)

    @pl.when(me_s < strip_n - 1)
    def _():
        halo_copy(0).wait_send()

    @pl.when(me_s > 0)
    def _():
        halo_copy(1).wait_send()

    settled(rs_v, strip_n - 1, 0)
    settled(tm_v, plane - 1, 2)
    settled(carry_v, len(planes) * strip_n - 1, 6)
    foot_load.wait()
    settled(all_v, (strip_n - 1) * share, 5)
    sums = []
    for h in halves:
        sums.append(smoothed(all_v[:, h].astype(F32) * col_v[QUALITY], h))
    settled(carry_v, len(planes) * strip_n - 1, 7)
    carried = carry_v[0]
    for i in range(1, len(planes) * strip_n):
        carried = carried + carry_v[i]
    for i, h in enumerate(halves):
        j = len(halves) + i
        value = sums[i] + prefix_v[:, h] * carried[i : i + 1] + suffix_v[:, h] * carried[j : j + 1]
        value = value * scale_v[:, h]
        act_v[:, h] = value
        low_v[:, h] = value.astype(BF16)

    settled(all_v, (strip_n - 1) * share, 4)


def rebuild(low_v, warp_v, foot_v, act_v, act_h, res_h, res_v, turned_v, sem):
    pixels = warp_v.shape[1]
    tile, wide = 512, 512
    copies = []
    low = low_v[...]
    for at in range(0, pixels, wide):
        for n in range(at, at + wide, tile):
            n = slice(n, n + tile)
            rebuilt = jnp.dot(low, foot_v[:, n], preferred_element_type=F32)
            res_v[:, n] = (warp_v[:, n].astype(F32) - rebuilt).astype(BF16)
        part = pl.ds(at, wide)
        copy = pltpu.make_async_copy(res_v.at[:, part], res_h.at[:, part], sem.at[1 + at // wide])
        copy.start()
        copies.append(copy)
        if at == 4 * wide:
            per = act_h.shape[0]
            for at in range(0, act_v.shape[1], 128):
                turned_v[at : at + 128] = act_v[:, at : at + 128].T
            mine = pl.ds(pl.multiple_of(lax.axis_index("strip") * per, per), per)
            copies.append(pltpu.make_async_copy(turned_v.at[mine], act_h, sem.at[0]))
            copies[-1].start()
    for copy in copies:
        copy.wait()


def body(tm_n, strip_n, movie, shifts, projection, footprints, quality, continuity, retention):
    frames, pixels = movie.shape
    factors = projection.shape[1]
    rows = shifts.shape[1]
    cols = pixels // rows
    per = factors // strip_n
    share = frames // strip_n
    halves = factors // 128
    steps = frames.bit_length() - 1
    DMA = pltpu.SemaphoreType.DMA
    vmem = pl.BlockSpec(memory_space=pltpu.VMEM)
    hbm = pl.BlockSpec(memory_space=pltpu.HBM)
    low, warped, foot, act = pl.pallas_call(
        functools.partial(kernel, tm_n, strip_n),
        out_shape=(
            pltpu.VMEM((frames, factors), BF16),
            pltpu.VMEM((frames, pixels), BF16),
            pltpu.VMEM((factors, pixels), BF16),
            pltpu.VMEM((frames, factors), F32),
        ),
        in_specs=[hbm] * 7,
        out_specs=(vmem,) * 4,
        scratch_shapes=[
            pltpu.VMEM((frames, pixels), BF16),
            pltpu.VMEM((pixels, factors), BF16),
            pltpu.VMEM((2, frames, cols), BF16),
            pltpu.VMEM((rows, frames, 128), F32),
            pltpu.VMEM((rows, frames), F32),
            pltpu.VMEM((tm_n, frames), F32),
            pltpu.VMEM((tm_n, frames), F32),
            pltpu.VMEM((1, factors), F32),
            pltpu.VMEM((2 * steps + 4, frames, 128), F32),
            pltpu.VMEM((4, tm_n, frames), F32),
            pltpu.VMEM((frames, factors), F32),
            pltpu.VMEM((frames, factors), F32),
            pltpu.VMEM((frames, factors), F32),
            pltpu.VMEM((2, 2 * halves, Z * CORES, 128), F32),
            pltpu.VMEM((frames, factors), F32),
            pltpu.VMEM((strip_n, share, factors), BF16),
            pltpu.VMEM((frames, factors), BF16),
            pltpu.VMEM((Z * CORES, 2 * halves, 128), F32),
            pltpu.VMEM((2 * strip_n, 2 * halves, 128), F32),
            DMA((9,)), DMA((2,)), DMA((2,)),
            DMA((8,)),
            pltpu.VMEM((2 * halves, 128), F32),
            pltpu.VMEM((frames, factors), BF16),
            pltpu.VMEM((2, 2 * halves, 128), F32),
            pltpu.VMEM((2 * halves, tm_n, 128), F32),
            pltpu.SemaphoreType.REGULAR((ROUNDS,)),
        ],
        compiler_params=pltpu.CompilerParams(
            collective_id=0, has_side_effects=True, vmem_limit_bytes=32 << 20
        ),
    )(
        *(
            pltpu.with_memory_space_constraint(x, pltpu.HBM)
            for x in (
                movie, shifts.T, projection, footprints,
                quality.reshape(tm_n, frames), continuity.reshape(tm_n, frames),
                retention.reshape(1, factors),
            )
        )
    )
    return pl.pallas_call(
        rebuild,
        out_shape=(
            jax.ShapeDtypeStruct((per, frames), F32),
            jax.ShapeDtypeStruct((frames, pixels), BF16),
        ),
        in_specs=[vmem] * 4,
        out_specs=(hbm, hbm),
        scratch_shapes=[
            pltpu.VMEM((frames, pixels), BF16),
            pltpu.VMEM((factors, frames), F32),
            DMA((1 + pixels // 512,)),
        ],
        compiler_params=pltpu.CompilerParams(vmem_limit_bytes=16 << 20),
    )(low, warped, foot, act)


def solution(mesh):
    return jax.shard_map(
        functools.partial(body, mesh.shape["tm"], mesh.shape["strip"]),
        mesh=mesh,
        in_specs=(
            P("tm", "strip"), P("tm", "strip"), P("strip", None), P(None, "strip"), P(), P(), P(),
        ),
        out_specs=(P("strip", "tm"), P("tm", "strip")),
        check_vma=False,
    )
```

```python
import functools

import jax
import jax.numpy as jnp
from jax import lax
from jax.experimental import pallas as pl
from jax.experimental.pallas import tpu as pltpu
from jax.sharding import PartitionSpec as P

MESH = pl.DeviceIdType.MESH
HI = lax.Precision.HIGHEST
F32 = jnp.float32
BF16 = jnp.bfloat16
Z, CORES, Y = 8, 2, 4
ROUNDS = 3


def lane_shift(x, d, fill):
    n = x.shape[1]
    lane = lax.broadcasted_iota(jnp.int32, x.shape, 1)
    keep = lane >= d if d > 0 else lane < n + d
    return jnp.where(keep, pltpu.roll(x, d % n, 1), fill)


def row_shift(x, d, fill):
    n = x.shape[0]
    row = lax.broadcasted_iota(jnp.int32, x.shape, 0)
    keep = row >= d if d > 0 else row < n + d
    return jnp.where(keep, pltpu.roll(x, d % n, 0), fill)


def row_turn(x, d):
    n = x.shape[0]
    d = d % n
    if d % 8 == 0:
        return jnp.concatenate([x[n - d :], x[: n - d]], axis=0)
    return pltpu.roll(x, d, 0)


def kernel(
    tm_n, strip_n,
    movie_h, shifts_h, proj_h, foot_h, quality_h, cont_h, ret_h,
    low_v, warp_v, foot_v, act_v,
    movie_v, proj_v, halo_v, shift_v, shifts_r, quality_r, cont_r, ret_r,
    col_v, rows_v, prefix_v, suffix_v, scale_v, coef_v, part_v,
    rs_v, all_v, tm_v, carry_v, out_v,
    load_sem, halo_send, halo_recv, sems, ends_v, sent_v, enter_v, table_v, step_v, round_sem,
):
    frames, pixels = movie_v.shape
    factors = proj_v.shape[1]
    rows = shifts_r.shape[0]
    cols = pixels // rows
    share = frames // strip_n
    steps = frames.bit_length() - 1
    me_t = lax.axis_index("tm")
    me_s = lax.axis_index("strip")
    halves = [slice(i, i + 128) for i in range(0, factors, 128)]

    barrier = pltpu.get_barrier_semaphore()
    plane = Z * CORES
    other_x = lax.rem(me_t + plane, 2 * plane)
    flip = 1 - 2 * lax.rem(me_t, CORES)
    corner = me_s // Y * Y
    planes = [me_t, other_x]
    place = lax.rem(me_t, plane)
    near = [
        {"tm": other_x},
        {"tm": other_x, "strip": lax.rem(me_s + Y, 2 * Y)},
        {"strip": corner + lax.rem(me_s + 1, Y)},
        {"strip": corner + lax.rem(me_s + Y - 1, Y)},
        {"tm": me_t // plane * plane + lax.rem(me_t + CORES, plane)},
        {"tm": me_t // plane * plane + lax.rem(me_t + plane - CORES, plane)},
    ]
    pair = [{"tm": me_t + flip}] + [{"tm": one["tm"] + flip} for one in near[4:]]

    def hail(sem, partners):
        for partner in partners:
            pl.semaphore_signal(sem, inc=1, device_id=partner, device_id_type=MESH)

    @pl.when(me_s == Y - 1)
    def _():
        hail(barrier, [{"strip": Y}])

    @pl.when(me_s == Y)
    def _():
        hail(barrier, [{"strip": Y - 1}])

    hail(barrier, near + pair)

    def next_round(n):
        if n:
            pl.semaphore_wait(round_sem.at[n - 1], len(near))
        if n < ROUNDS:
            hail(round_sem.at[n], near)

    small = [
        pltpu.make_async_copy(source, target, load_sem.at[i])
        for i, (source, target) in enumerate(
            ((shifts_h, shifts_r), (quality_h, quality_r), (cont_h, cont_r), (ret_h, ret_r))
        )
    ]
    large = [
        pltpu.make_async_copy(movie_h, movie_v, load_sem.at[4]),
        pltpu.make_async_copy(proj_h, proj_v, load_sem.at[5]),
    ]
    foot_load = pltpu.make_async_copy(foot_h, foot_v, load_sem.at[6])
    for copy in small + large:
        copy.start()
    crossing = (me_s == Y - 1) | (me_s == Y)

    @pl.when(crossing)
    def _():
        pl.semaphore_wait(barrier, len(near) + len(pair) + 1)

    @pl.when(jnp.logical_not(crossing))
    def _():
        pl.semaphore_wait(barrier, len(near) + len(pair))

    def halo_copy(side):
        source = pl.ds((rows - 1) * cols, cols) if side == 0 else pl.ds(0, cols)
        target = me_s + 1 if side == 0 else me_s - 1
        return pltpu.make_async_remote_copy(
            src_ref=movie_h.at[:, source], dst_ref=halo_v.at[side],
            send_sem=halo_send.at[side], recv_sem=halo_recv.at[side],
            device_id={"strip": target}, device_id_type=MESH,
        )

    @pl.when(me_s < strip_n - 1)
    def _():
        halo_copy(0).start()

    @pl.when(me_s > 0)
    def _():
        halo_copy(1).start()

    @pl.when(me_s == 0)
    def _():
        halo_v[0] = jnp.zeros((frames, cols), BF16)

    @pl.when(me_s == strip_n - 1)
    def _():
        halo_v[1] = jnp.zeros((frames, cols), BF16)

    next_round(0)
    for copy in small:
        copy.wait()

    shifts = jnp.concatenate([shifts_r[...], jnp.zeros((frames - rows, frames), F32)], axis=0).T
    for h in range(rows):
        shift_v[h] = jnp.broadcast_to(shifts[:, h : h + 1], (frames, 128))

    quality, cont = quality_r[...], cont_r[...]
    ret = ret_r[...]
    powers = [ret]
    for _ in range(steps):
        powers.append(powers[-1] * powers[-1])
    prefix, suffix = cont, cont
    for level in range(steps):
        d = 1 << level
        prefix = prefix * lane_shift(prefix, d, 1.0)
        suffix = suffix * lane_shift(suffix, -d, 1.0)
    after = lane_shift(suffix, -1, 1.0)
    next_round(1)
    rows_v[0] = quality
    rows_v[1] = cont
    rows_v[2] = prefix
    rows_v[3] = after
    mine = [rows_v[i, pl.ds(me_t, 1), :] for i in range(4)]
    lane = lax.broadcasted_iota(jnp.int32, (1, frames), 1)
    ahead, behind = mine[1], mine[1]
    ahead_rows, behind_rows = [], []
    for level in range(steps):
        d = 1 << level
        ahead_rows.append(jnp.where(lane >= d, ahead, 0.0))
        behind_rows.append(jnp.where(lane < frames - d, behind, 0.0))
        ahead = ahead * lane_shift(ahead, d, 1.0)
        behind = behind * lane_shift(behind, -d, 1.0)
    lines = ahead_rows + behind_rows + mine
    lines = jnp.concatenate(lines + [jnp.zeros((frames - len(lines), frames), F32)], axis=0)
    turned = lines.T
    for i in range(2 * steps + 4):
        col_v[i] = jnp.broadcast_to(turned[:, i : i + 1], (frames, 128))
    QUALITY, CONT, PREFIX, AFTER = (2 * steps + i for i in range(4))

    small = [jnp.ones_like(ret), ret, powers[1], powers[1] * ret, powers[2]]
    small += [powers[2] * small[i] for i in (1, 2, 3)]
    rising = jnp.concatenate(small[1:] + [powers[3]], axis=0)
    falling = jnp.concatenate(small[::-1], axis=0)
    for level in range(3, steps):
        rising = jnp.concatenate([rising, rising * powers[level]], axis=0)
        falling = jnp.concatenate([falling * powers[level], falling], axis=0)
    for h in halves:
        prefix_v[:, h] = col_v[PREFIX] * rising[:, h]
        suffix_v[:, h] = col_v[AFTER] * falling[:, h]

    def warp_row(h, above, own, below):
        s = shift_v[h]
        near = jnp.abs(s)
        keep = jnp.maximum(0.0, 1.0 - near)
        down = s > 0.0
        for w in range(0, cols, 128):
            w = slice(w, w + 128)
            other = jnp.where(down, below[:, w].astype(F32), above[:, w].astype(F32))
            warped = keep * own[:, w].astype(F32) + near * other
            yield w, warped.astype(BF16)

    def row_ref(h):
        return movie_v.at[:, h * cols : (h + 1) * cols]

    def warp_into(h, above, below):
        for w, warped in warp_row(h, above[...], row_ref(h)[...], below[...]):
            warp_v[:, h * cols + w.start : h * cols + w.stop] = warped

    def project(first, last):
        at = slice(first * cols, last * cols)
        return jnp.dot(warp_v[:, at], proj_v[at, :], preferred_element_type=F32)

    next_round(2)
    for copy in large:
        copy.wait()
    group = 4
    for first in range(1, rows - 1, group):
        last = min(first + group, rows - 1)
        for h in range(first, last):
            warp_into(h, row_ref(h - 1), row_ref(h + 1))
        inner = project(first, last)
        part_v[...] = inner if first == 1 else part_v[...] + inner
        if first == 1 + 2 * group:
            next_round(3)
    foot_load.start()

    swap = me_s // Y - me_s // (Y + 1)

    def edge(n, _):
        side = lax.rem(n + swap, 2)

        @pl.when(me_s + side * (strip_n - 1) - me_s * side * 2 > 0)
        def _():
            pltpu.make_async_copy(halo_v.at[side], halo_v.at[side], halo_recv.at[side]).wait()

        at = pl.multiple_of(side * (rows - 1) * cols, cols)
        inner = pl.multiple_of((1 + side * (rows - 3)) * cols, cols)
        s = shift_v[side * (rows - 1)]
        near_weight = jnp.abs(s)
        keep = jnp.maximum(0.0, 1.0 - near_weight)
        outside = s * (2 * side - 1).astype(F32) > 0.0
        for w in range(0, cols, 128):
            other = jnp.where(
                outside,
                halo_v[side, :, w : w + 128].astype(F32),
                movie_v[:, pl.ds(inner + w, 128)].astype(F32),
            )
            own = movie_v[:, pl.ds(at + w, 128)].astype(F32)
            warp_v[:, pl.ds(at + w, 128)] = (keep * own + near_weight * other).astype(BF16)
        part_v[...] += jnp.dot(
            warp_v[:, pl.ds(at, cols)], proj_v[pl.ds(at, cols), :], preferred_element_type=F32
        )
        return 0

    lax.fori_loop(0, 2, edge, 0)

    def strip_peer(d):
        return lax.rem(me_s + d, strip_n)

    def rs_copy(peer):
        return pltpu.make_async_remote_copy(
            src_ref=sent_v.at[pl.ds(pl.multiple_of(peer * share, share), share)],
            dst_ref=rs_v.at[me_s], send_sem=sems.at[0], recv_sem=sems.at[1],
            device_id={"strip": peer}, device_id_type=MESH,
        )

    def tm_copy(peer):
        return pltpu.make_async_remote_copy(
            src_ref=ends_v, dst_ref=tm_v.at[place], send_sem=sems.at[2], recv_sem=sems.at[3],
            device_id={"tm": me_t // plane * plane + peer}, device_id_type=MESH,
        )

    def ag_copy(peer):
        mine = pl.ds(pl.multiple_of(me_s * share, share), share)
        return pltpu.make_async_remote_copy(
            src_ref=all_v.at[mine], dst_ref=all_v.at[mine],
            send_sem=sems.at[4], recv_sem=sems.at[5],
            device_id={"strip": peer}, device_id_type=MESH,
        )

    def cs_copy(j, peer):
        slot = j * strip_n + me_s
        return pltpu.make_async_remote_copy(
            src_ref=enter_v.at[j], dst_ref=carry_v.at[slot],
            send_sem=sems.at[6], recv_sem=sems.at[7],
            device_id={"tm": planes[j], "strip": peer}, device_id_type=MESH,
        )

    for i, h in enumerate(halves):
        weighted = part_v[:, h] * col_v[QUALITY]
        j = len(halves) + i
        ends_v[i : i + 1] = jnp.sum(weighted * suffix_v[:, h], axis=0, keepdims=True)
        ends_v[j : j + 1] = jnp.sum(weighted * prefix_v[:, h], axis=0, keepdims=True)
    tm_v[place] = ends_v[...]
    for dz in (4, 3, 5, 2, 6, 1, 7, 0):
        for dc in (1, 0):
            if dz or dc:
                other = lax.rem(place // CORES + dz, Z) * CORES + lax.rem(place + dc, CORES)
                tm_copy(other).start()
    sent_v[...] = part_v[...].astype(BF16)
    peers = [
        lax.rem(me_s // Y + dx, 2) * Y + lax.rem(me_s + dy, Y)
        for dx, dy in ((1, 2), (1, 1), (1, 3), (0, 2), (1, 0), (0, 1), (0, 3))
    ]
    for peer in peers:
        rs_copy(peer).start()

    def settled(ref, count, i):
        part = ref.at[pl.ds(0, count)]
        pltpu.make_async_copy(part, part, sems.at[i]).wait()

    whole = prefix[:, frames - 1 : frames] * powers[steps]
    block = lax.broadcasted_iota(jnp.int32, (tm_n, factors), 0)
    mine = pl.ds(pl.multiple_of(me_t // plane * plane, plane), plane)
    for j, target in enumerate(planes):
        before = jnp.where(block < target, whole, 1.0)
        beyond = jnp.where(block > target, whole, 1.0)
        d = 1
        while d < tm_n:
            before = before * row_shift(before, -d, 1.0)
            beyond = beyond * row_shift(beyond, d, 1.0)
            d *= 2
        before = jnp.where(block < target, row_shift(before, -1, 1.0), 0.0)
        beyond = jnp.where(block > target, row_shift(beyond, 1, 1.0), 0.0)
        for i, h in enumerate(halves):
            table_v[i] = before[:, h]
            table_v[len(halves) + i] = beyond[:, h]
        for i in range(2 * len(halves)):
            coef_v[j, i] = table_v[i, mine, :]
        if j == 0:
            norm_in = jnp.sum(
                before
                * jnp.dot(quality * after, falling, precision=HI, preferred_element_type=F32),
                axis=0, keepdims=True,
            )
            norm_out = jnp.sum(
                beyond
                * jnp.dot(quality * prefix, rising, precision=HI, preferred_element_type=F32),
                axis=0, keepdims=True,
            )

    rs_v[me_s] = jnp.zeros((share, factors), BF16)
    settled(rs_v, strip_n - 1, 1)
    total = part_v[pl.ds(pl.multiple_of(me_s * share, share), share), :]
    for i in range(strip_n):
        total = total + rs_v[i].astype(F32)
    all_v[pl.ds(pl.multiple_of(me_s * share, share), share), :] = total.astype(BF16)
    for peer in peers:
        ag_copy(peer).start()

    settled(tm_v, plane - 1, 3)
    for i in range(2 * len(halves)):
        ends = tm_v[:, i, :]
        for j in range(len(planes)):
            enter_v[j, i : i + 1] = jnp.sum(coef_v[j, i] * ends, axis=0, keepdims=True)
    carry_v[me_s] = enter_v[0]
    for j in (1, 0):
        for peer in peers + [me_s] * j:
            cs_copy(j, peer).start()
    for h in halves:
        for level in range(steps):
            step_v[level, :, h] = col_v[level] * powers[level][:, h]
            step_v[steps + level, :, h] = col_v[steps + level] * powers[level][:, h]

    def smoothed(x, h):
        fore = x
        back = x * (col_v[CONT] * ret[:, h])
        for level in range(steps):
            d = 1 << level
            fore = fore + step_v[level, :, h] * row_turn(fore, d)
            back = back + step_v[steps + level, :, h] * row_turn(back, -d)
        row = lax.broadcasted_iota(jnp.int32, back.shape, 0)
        return fore + jnp.where(row < frames - 1, row_turn(back, -1), 0.0)

    for h in halves:
        norm = smoothed(col_v[QUALITY], h)
        norm = norm + prefix_v[:, h] * norm_in[:, h] + suffix_v[:, h] * norm_out[:, h]
        scale = 1.0 / jnp.sqrt(norm)
        scale_v[:, h] = scale
        prefix_v[:, h] *= scale
        suffix_v[:, h] *= scale

    @pl.when(me_s < strip_n - 1)
    def _():
        halo_copy(0).wait_send()

    @pl.when(me_s > 0)
    def _():
        halo_copy(1).wait_send()

    settled(rs_v, strip_n - 1, 0)
    settled(tm_v, plane - 1, 2)
    settled(carry_v, len(planes) * strip_n - 1, 6)
    foot_load.wait()
    settled(all_v, (strip_n - 1) * share, 5)
    sums = []
    for h in halves:
        sums.append(smoothed(all_v[:, h].astype(F32) * col_v[QUALITY], h) * scale_v[:, h])
    settled(carry_v, len(planes) * strip_n - 1, 7)
    carried = carry_v[0]
    for i in range(1, len(planes) * strip_n):
        carried = carried + carry_v[i]
    for i, h in enumerate(halves):
        j = len(halves) + i
        value = sums[i] + prefix_v[:, h] * carried[i : i + 1] + suffix_v[:, h] * carried[j : j + 1]
        out_v[h, :] = value.T
        low_v[:, h] = value.astype(BF16)
    per = factors // strip_n
    act_v[...] = out_v[pl.ds(pl.multiple_of(me_s * per, per), per), :]

    settled(all_v, (strip_n - 1) * share, 4)


def rebuild(low_v, warp_v, foot_v, act_v, act_h, res_h, res_v, sem):
    pixels = warp_v.shape[1]
    tile, wide = 512, 512
    copies = [pltpu.make_async_copy(act_v, act_h, sem.at[0])]
    copies[0].start()
    low = low_v[...]
    for at in range(0, pixels, wide):
        for n in range(at, at + wide, tile):
            n = slice(n, n + tile)
            rebuilt = jnp.dot(low, foot_v[:, n], preferred_element_type=F32)
            res_v[:, n] = (warp_v[:, n].astype(F32) - rebuilt).astype(BF16)
        part = pl.ds(at, wide)
        copy = pltpu.make_async_copy(res_v.at[:, part], res_h.at[:, part], sem.at[1 + at // wide])
        copy.start()
        copies.append(copy)
    for copy in copies:
        copy.wait()


def body(tm_n, strip_n, movie, shifts, projection, footprints, quality, continuity, retention):
    frames, pixels = movie.shape
    factors = projection.shape[1]
    rows = shifts.shape[1]
    cols = pixels // rows
    per = factors // strip_n
    share = frames // strip_n
    halves = factors // 128
    steps = frames.bit_length() - 1
    DMA = pltpu.SemaphoreType.DMA
    vmem = pl.BlockSpec(memory_space=pltpu.VMEM)
    hbm = pl.BlockSpec(memory_space=pltpu.HBM)
    low, warped, foot, act = pl.pallas_call(
        functools.partial(kernel, tm_n, strip_n),
        out_shape=(
            pltpu.VMEM((frames, factors), BF16),
            pltpu.VMEM((frames, pixels), BF16),
            pltpu.VMEM((factors, pixels), BF16),
            pltpu.VMEM((per, frames), F32),
        ),
        in_specs=[hbm] * 7,
        out_specs=(vmem,) * 4,
        scratch_shapes=[
            pltpu.VMEM((frames, pixels), BF16),
            pltpu.VMEM((pixels, factors), BF16),
            pltpu.VMEM((2, frames, cols), BF16),
            pltpu.VMEM((rows, frames, 128), F32),
            pltpu.VMEM((rows, frames), F32),
            pltpu.VMEM((tm_n, frames), F32),
            pltpu.VMEM((tm_n, frames), F32),
            pltpu.VMEM((1, factors), F32),
            pltpu.VMEM((2 * steps + 4, frames, 128), F32),
            pltpu.VMEM((4, tm_n, frames), F32),
            pltpu.VMEM((frames, factors), F32),
            pltpu.VMEM((frames, factors), F32),
            pltpu.VMEM((frames, factors), F32),
            pltpu.VMEM((2, 2 * halves, Z * CORES, 128), F32),
            pltpu.VMEM((frames, factors), F32),
            pltpu.VMEM((strip_n, share, factors), BF16),
            pltpu.VMEM((frames, factors), BF16),
            pltpu.VMEM((Z * CORES, 2 * halves, 128), F32),
            pltpu.VMEM((2 * strip_n, 2 * halves, 128), F32),
            pltpu.VMEM((factors, frames), F32),
            DMA((7,)), DMA((2,)), DMA((2,)),
            DMA((8,)),
            pltpu.VMEM((2 * halves, 128), F32),
            pltpu.VMEM((frames, factors), BF16),
            pltpu.VMEM((2, 2 * halves, 128), F32),
            pltpu.VMEM((2 * halves, tm_n, 128), F32),
            pltpu.VMEM((2 * steps, frames, factors), F32),
            pltpu.SemaphoreType.REGULAR((ROUNDS,)),
        ],
        compiler_params=pltpu.CompilerParams(
            collective_id=0, has_side_effects=True, vmem_limit_bytes=32 << 20
        ),
    )(
        *(
            pltpu.with_memory_space_constraint(x, pltpu.HBM)
            for x in (
                movie, shifts.T, projection, footprints,
                quality.reshape(tm_n, frames), continuity.reshape(tm_n, frames),
                retention.reshape(1, factors),
            )
        )
    )
    return pl.pallas_call(
        rebuild,
        out_shape=(
            jax.ShapeDtypeStruct((per, frames), F32),
            jax.ShapeDtypeStruct((frames, pixels), BF16),
        ),
        in_specs=[vmem] * 4,
        out_specs=(hbm, hbm),
        scratch_shapes=[pltpu.VMEM((frames, pixels), BF16), DMA((1 + pixels // 512,))],
        compiler_params=pltpu.CompilerParams(vmem_limit_bytes=16 << 20),
    )(low, warped, foot, act)


def solution(mesh):
    return jax.shard_map(
        functools.partial(body, mesh.shape["tm"], mesh.shape["strip"]),
        mesh=mesh,
        in_specs=(
            P("tm", "strip"), P("tm", "strip"), P("strip", None), P(None, "strip"), P(), P(), P(),
        ),
        out_specs=(P("strip", "tm"), P("tm", "strip")),
        check_vma=False,
    )
```

```python
import functools

import jax
import jax.numpy as jnp
from jax import lax
from jax.experimental import pallas as pl
from jax.experimental.pallas import tpu as pltpu
from jax.sharding import PartitionSpec as P

MESH = pl.DeviceIdType.MESH
HI = lax.Precision.HIGHEST
F32 = jnp.float32
BF16 = jnp.bfloat16
Z, CORES, Y = 8, 2, 4
ROUNDS = 3


def lane_shift(x, d, fill):
    n = x.shape[1]
    lane = lax.broadcasted_iota(jnp.int32, x.shape, 1)
    keep = lane >= d if d > 0 else lane < n + d
    return jnp.where(keep, pltpu.roll(x, d % n, 1), fill)


def row_shift(x, d, fill):
    n = x.shape[0]
    row = lax.broadcasted_iota(jnp.int32, x.shape, 0)
    keep = row >= d if d > 0 else row < n + d
    return jnp.where(keep, pltpu.roll(x, d % n, 0), fill)


def row_turn(x, d):
    n = x.shape[0]
    d = d % n
    if d % 8 == 0:
        return jnp.concatenate([x[n - d :], x[: n - d]], axis=0)
    return pltpu.roll(x, d, 0)


def kernel(
    tm_n, strip_n,
    movie_h, shifts_h, proj_h, foot_h, quality_h, cont_h, ret_h,
    low_v, warp_v, foot_v, act_v,
    movie_v, proj_v, halo_v, shift_v, shifts_r, quality_r, cont_r, ret_r,
    col_v, rows_v, prefix_v, suffix_v, scale_v, coef_v, part_v,
    rs_v, all_v, tm_v, carry_v, out_v,
    load_sem, halo_send, halo_recv, sems, ends_v, sent_v, enter_v, table_v, round_sem,
):
    frames, pixels = movie_v.shape
    factors = proj_v.shape[1]
    rows = shifts_r.shape[0]
    cols = pixels // rows
    share = frames // strip_n
    steps = frames.bit_length() - 1
    me_t = lax.axis_index("tm")
    me_s = lax.axis_index("strip")
    halves = [slice(i, i + 128) for i in range(0, factors, 128)]

    barrier = pltpu.get_barrier_semaphore()
    plane = Z * CORES
    other_x = lax.rem(me_t + plane, 2 * plane)
    flip = 1 - 2 * lax.rem(me_t, CORES)
    corner = me_s // Y * Y
    planes = [me_t, other_x]
    place = lax.rem(me_t, plane)
    near = [
        {"tm": other_x},
        {"tm": other_x, "strip": lax.rem(me_s + Y, 2 * Y)},
        {"strip": corner + lax.rem(me_s + 1, Y)},
        {"strip": corner + lax.rem(me_s + Y - 1, Y)},
        {"tm": me_t // plane * plane + lax.rem(me_t + CORES, plane)},
        {"tm": me_t // plane * plane + lax.rem(me_t + plane - CORES, plane)},
    ]
    pair = [{"tm": me_t + flip}] + [{"tm": one["tm"] + flip} for one in near[4:]]

    def hail(sem, partners):
        for partner in partners:
            pl.semaphore_signal(sem, inc=1, device_id=partner, device_id_type=MESH)

    @pl.when(me_s == Y - 1)
    def _():
        hail(barrier, [{"strip": Y}])

    @pl.when(me_s == Y)
    def _():
        hail(barrier, [{"strip": Y - 1}])

    hail(barrier, near + pair)

    def next_round(n):
        if n:
            pl.semaphore_wait(round_sem.at[n - 1], len(near))
        if n < ROUNDS:
            hail(round_sem.at[n], near)

    small = [
        pltpu.make_async_copy(source, target, load_sem.at[i])
        for i, (source, target) in enumerate(
            ((shifts_h, shifts_r), (quality_h, quality_r), (cont_h, cont_r), (ret_h, ret_r))
        )
    ]
    large = [
        pltpu.make_async_copy(movie_h, movie_v, load_sem.at[4]),
        pltpu.make_async_copy(proj_h, proj_v, load_sem.at[5]),
    ]
    foot_load = pltpu.make_async_copy(foot_h, foot_v, load_sem.at[6])
    for copy in small + large:
        copy.start()
    crossing = (me_s == Y - 1) | (me_s == Y)

    @pl.when(crossing)
    def _():
        pl.semaphore_wait(barrier, len(near) + len(pair) + 1)

    @pl.when(jnp.logical_not(crossing))
    def _():
        pl.semaphore_wait(barrier, len(near) + len(pair))

    def halo_copy(side):
        source = pl.ds((rows - 1) * cols, cols) if side == 0 else pl.ds(0, cols)
        target = me_s + 1 if side == 0 else me_s - 1
        return pltpu.make_async_remote_copy(
            src_ref=movie_h.at[:, source], dst_ref=halo_v.at[side],
            send_sem=halo_send.at[side], recv_sem=halo_recv.at[side],
            device_id={"strip": target}, device_id_type=MESH,
        )

    @pl.when(me_s < strip_n - 1)
    def _():
        halo_copy(0).start()

    @pl.when(me_s > 0)
    def _():
        halo_copy(1).start()

    @pl.when(me_s == 0)
    def _():
        halo_v[0] = jnp.zeros((frames, cols), BF16)

    @pl.when(me_s == strip_n - 1)
    def _():
        halo_v[1] = jnp.zeros((frames, cols), BF16)

    next_round(0)
    for copy in small:
        copy.wait()

    shifts = jnp.concatenate([shifts_r[...], jnp.zeros((frames - rows, frames), F32)], axis=0).T
    for h in range(rows):
        shift_v[h] = jnp.broadcast_to(shifts[:, h : h + 1], (frames, 128))

    quality, cont = quality_r[...], cont_r[...]
    ret = ret_r[...]
    powers = [ret]
    for _ in range(steps):
        powers.append(powers[-1] * powers[-1])
    prefix, suffix = cont, cont
    for level in range(steps):
        d = 1 << level
        prefix = prefix * lane_shift(prefix, d, 1.0)
        suffix = suffix * lane_shift(suffix, -d, 1.0)
    after = lane_shift(suffix, -1, 1.0)
    rows_v[0] = quality
    rows_v[1] = cont
    rows_v[2] = prefix
    rows_v[3] = after
    mine = [rows_v[i, pl.ds(me_t, 1), :] for i in range(4)]
    lane = lax.broadcasted_iota(jnp.int32, (1, frames), 1)
    ahead, behind = mine[1], mine[1]
    ahead_rows, behind_rows = [], []
    for level in range(steps):
        d = 1 << level
        ahead_rows.append(jnp.where(lane >= d, ahead, 0.0))
        behind_rows.append(jnp.where(lane < frames - d, behind, 0.0))
        ahead = ahead * lane_shift(ahead, d, 1.0)
        behind = behind * lane_shift(behind, -d, 1.0)
    lines = ahead_rows + behind_rows + mine
    lines = jnp.concatenate(lines + [jnp.zeros((frames - len(lines), frames), F32)], axis=0)
    turned = lines.T
    for i in range(2 * steps + 4):
        col_v[i] = jnp.broadcast_to(turned[:, i : i + 1], (frames, 128))
    QUALITY, CONT, PREFIX, AFTER = (2 * steps + i for i in range(4))

    small = [jnp.ones_like(ret), ret, powers[1], powers[1] * ret, powers[2]]
    small += [powers[2] * small[i] for i in (1, 2, 3)]
    rising = jnp.concatenate(small[1:] + [powers[3]], axis=0)
    falling = jnp.concatenate(small[::-1], axis=0)
    for level in range(3, steps):
        rising = jnp.concatenate([rising, rising * powers[level]], axis=0)
        falling = jnp.concatenate([falling * powers[level], falling], axis=0)
    for h in halves:
        prefix_v[:, h] = col_v[PREFIX] * rising[:, h]
        suffix_v[:, h] = col_v[AFTER] * falling[:, h]

    def warp_row(h, above, own, below):
        s = shift_v[h]
        near = jnp.abs(s)
        keep = jnp.maximum(0.0, 1.0 - near)
        down = s > 0.0
        for w in range(0, cols, 128):
            w = slice(w, w + 128)
            other = jnp.where(down, below[:, w].astype(F32), above[:, w].astype(F32))
            warped = keep * own[:, w].astype(F32) + near * other
            yield w, warped.astype(BF16)

    def row_ref(h):
        return movie_v.at[:, h * cols : (h + 1) * cols]

    def warp_into(h, above, below):
        for w, warped in warp_row(h, above[...], row_ref(h)[...], below[...]):
            warp_v[:, h * cols + w.start : h * cols + w.stop] = warped

    def project(first, last):
        at = slice(first * cols, last * cols)
        return jnp.dot(warp_v[:, at], proj_v[at, :], preferred_element_type=F32)

    next_round(1)
    for copy in large:
        copy.wait()
    group = 4
    for first in range(1, rows - 1, group):
        last = min(first + group, rows - 1)
        for h in range(first, last):
            warp_into(h, row_ref(h - 1), row_ref(h + 1))
        inner = project(first, last)
        part_v[...] = inner if first == 1 else part_v[...] + inner
    next_round(2)
    foot_load.start()

    swap = me_s // Y - me_s // (Y + 1)

    def edge(n, _):
        side = lax.rem(n + swap, 2)

        @pl.when(me_s + side * (strip_n - 1) - me_s * side * 2 > 0)
        def _():
            pltpu.make_async_copy(halo_v.at[side], halo_v.at[side], halo_recv.at[side]).wait()

        at = pl.multiple_of(side * (rows - 1) * cols, cols)
        inner = pl.multiple_of((1 + side * (rows - 3)) * cols, cols)
        s = shift_v[side * (rows - 1)]
        near_weight = jnp.abs(s)
        keep = jnp.maximum(0.0, 1.0 - near_weight)
        outside = s * (2 * side - 1).astype(F32) > 0.0
        for w in range(0, cols, 128):
            other = jnp.where(
                outside,
                halo_v[side, :, w : w + 128].astype(F32),
                movie_v[:, pl.ds(inner + w, 128)].astype(F32),
            )
            own = movie_v[:, pl.ds(at + w, 128)].astype(F32)
            warp_v[:, pl.ds(at + w, 128)] = (keep * own + near_weight * other).astype(BF16)
        part_v[...] += jnp.dot(
            warp_v[:, pl.ds(at, cols)], proj_v[pl.ds(at, cols), :], preferred_element_type=F32
        )
        return 0

    lax.fori_loop(0, 2, edge, 0)

    def strip_peer(d):
        return lax.rem(me_s + d, strip_n)

    def rs_copy(peer):
        return pltpu.make_async_remote_copy(
            src_ref=sent_v.at[pl.ds(pl.multiple_of(peer * share, share), share)],
            dst_ref=rs_v.at[me_s], send_sem=sems.at[0], recv_sem=sems.at[1],
            device_id={"strip": peer}, device_id_type=MESH,
        )

    def tm_copy(peer):
        return pltpu.make_async_remote_copy(
            src_ref=ends_v, dst_ref=tm_v.at[place], send_sem=sems.at[2], recv_sem=sems.at[3],
            device_id={"tm": me_t // plane * plane + peer}, device_id_type=MESH,
        )

    def ag_copy(peer):
        mine = pl.ds(pl.multiple_of(me_s * share, share), share)
        return pltpu.make_async_remote_copy(
            src_ref=all_v.at[mine], dst_ref=all_v.at[mine],
            send_sem=sems.at[4], recv_sem=sems.at[5],
            device_id={"strip": peer}, device_id_type=MESH,
        )

    def cs_copy(j, peer):
        slot = j * strip_n + me_s
        return pltpu.make_async_remote_copy(
            src_ref=enter_v.at[j], dst_ref=carry_v.at[slot],
            send_sem=sems.at[6], recv_sem=sems.at[7],
            device_id={"tm": planes[j], "strip": peer}, device_id_type=MESH,
        )

    for i, h in enumerate(halves):
        weighted = part_v[:, h] * col_v[QUALITY]
        j = len(halves) + i
        ends_v[i : i + 1] = jnp.sum(weighted * suffix_v[:, h], axis=0, keepdims=True)
        ends_v[j : j + 1] = jnp.sum(weighted * prefix_v[:, h], axis=0, keepdims=True)
    tm_v[place] = ends_v[...]
    next_round(3)
    for dz in (4, 3, 5, 2, 6, 1, 7, 0):
        for dc in (1, 0):
            if dz or dc:
                other = lax.rem(place // CORES + dz, Z) * CORES + lax.rem(place + dc, CORES)
                tm_copy(other).start()
    sent_v[...] = part_v[...].astype(BF16)
    peers = [
        lax.rem(me_s // Y + dx, 2) * Y + lax.rem(me_s + dy, Y)
        for dx, dy in ((1, 2), (1, 1), (1, 3), (0, 2), (1, 0), (0, 1), (0, 3))
    ]
    for peer in peers:
        rs_copy(peer).start()

    def settled(ref, count, i):
        part = ref.at[pl.ds(0, count)]
        pltpu.make_async_copy(part, part, sems.at[i]).wait()

    whole = prefix[:, frames - 1 : frames] * powers[steps]
    block = lax.broadcasted_iota(jnp.int32, (tm_n, factors), 0)
    mine = pl.ds(pl.multiple_of(me_t // plane * plane, plane), plane)
    for j, target in enumerate(planes):
        before = jnp.where(block < target, whole, 1.0)
        beyond = jnp.where(block > target, whole, 1.0)
        d = 1
        while d < tm_n:
            before = before * row_shift(before, -d, 1.0)
            beyond = beyond * row_shift(beyond, d, 1.0)
            d *= 2
        before = jnp.where(block < target, row_shift(before, -1, 1.0), 0.0)
        beyond = jnp.where(block > target, row_shift(beyond, 1, 1.0), 0.0)
        for i, h in enumerate(halves):
            table_v[i] = before[:, h]
            table_v[len(halves) + i] = beyond[:, h]
        for i in range(2 * len(halves)):
            coef_v[j, i] = table_v[i, mine, :]
        if j == 0:
            norm_in = jnp.sum(
                before
                * jnp.dot(quality * after, falling, precision=HI, preferred_element_type=F32),
                axis=0, keepdims=True,
            )
            norm_out = jnp.sum(
                beyond
                * jnp.dot(quality * prefix, rising, precision=HI, preferred_element_type=F32),
                axis=0, keepdims=True,
            )

    rs_v[me_s] = jnp.zeros((share, factors), BF16)
    settled(rs_v, strip_n - 1, 1)
    total = part_v[pl.ds(pl.multiple_of(me_s * share, share), share), :]
    for i in range(strip_n):
        total = total + rs_v[i].astype(F32)
    all_v[pl.ds(pl.multiple_of(me_s * share, share), share), :] = total.astype(BF16)
    for peer in peers:
        ag_copy(peer).start()

    settled(tm_v, plane - 1, 3)
    for i in range(2 * len(halves)):
        ends = tm_v[:, i, :]
        for j in range(len(planes)):
            enter_v[j, i : i + 1] = jnp.sum(coef_v[j, i] * ends, axis=0, keepdims=True)
    carry_v[me_s] = enter_v[0]
    for j in (1, 0):
        for peer in peers + [me_s] * j:
            cs_copy(j, peer).start()
    def smoothed(x, h):
        fore = x
        back = x * (col_v[CONT] * ret[:, h])
        for level in range(steps):
            d = 1 << level
            fore = fore + (col_v[level] * powers[level][:, h]) * row_turn(fore, d)
            back = back + (col_v[steps + level] * powers[level][:, h]) * row_turn(back, -d)
        row = lax.broadcasted_iota(jnp.int32, back.shape, 0)
        return fore + jnp.where(row < frames - 1, row_turn(back, -1), 0.0)

    for h in halves:
        norm = smoothed(col_v[QUALITY], h)
        norm = norm + prefix_v[:, h] * norm_in[:, h] + suffix_v[:, h] * norm_out[:, h]
        scale_v[:, h] = 1.0 / jnp.sqrt(norm)

    @pl.when(me_s < strip_n - 1)
    def _():
        halo_copy(0).wait_send()

    @pl.when(me_s > 0)
    def _():
        halo_copy(1).wait_send()

    settled(rs_v, strip_n - 1, 0)
    settled(tm_v, plane - 1, 2)
    settled(carry_v, len(planes) * strip_n - 1, 6)
    foot_load.wait()
    settled(all_v, (strip_n - 1) * share, 5)
    sums = []
    for h in halves:
        sums.append(smoothed(all_v[:, h].astype(F32) * col_v[QUALITY], h))
    settled(carry_v, len(planes) * strip_n - 1, 7)
    carried = carry_v[0]
    for i in range(1, len(planes) * strip_n):
        carried = carried + carry_v[i]
    for i, h in enumerate(halves):
        j = len(halves) + i
        value = sums[i] + prefix_v[:, h] * carried[i : i + 1] + suffix_v[:, h] * carried[j : j + 1]
        value = value * scale_v[:, h]
        out_v[h, :] = value.T
        low_v[:, h] = value.astype(BF16)
    per = factors // strip_n
    act_v[...] = out_v[pl.ds(pl.multiple_of(me_s * per, per), per), :]

    settled(all_v, (strip_n - 1) * share, 4)


def rebuild(low_v, warp_v, foot_v, act_v, act_h, res_h, res_v, sem):
    pixels = warp_v.shape[1]
    tile, wide = 512, 512
    copies = [pltpu.make_async_copy(act_v, act_h, sem.at[0])]
    copies[0].start()
    low = low_v[...]
    for at in range(0, pixels, wide):
        for n in range(at, at + wide, tile):
            n = slice(n, n + tile)
            rebuilt = jnp.dot(low, foot_v[:, n], preferred_element_type=F32)
            res_v[:, n] = (warp_v[:, n].astype(F32) - rebuilt).astype(BF16)
        part = pl.ds(at, wide)
        copy = pltpu.make_async_copy(res_v.at[:, part], res_h.at[:, part], sem.at[1 + at // wide])
        copy.start()
        copies.append(copy)
    for copy in copies:
        copy.wait()


def body(tm_n, strip_n, movie, shifts, projection, footprints, quality, continuity, retention):
    frames, pixels = movie.shape
    factors = projection.shape[1]
    rows = shifts.shape[1]
    cols = pixels // rows
    per = factors // strip_n
    share = frames // strip_n
    halves = factors // 128
    steps = frames.bit_length() - 1
    DMA = pltpu.SemaphoreType.DMA
    vmem = pl.BlockSpec(memory_space=pltpu.VMEM)
    hbm = pl.BlockSpec(memory_space=pltpu.HBM)
    low, warped, foot, act = pl.pallas_call(
        functools.partial(kernel, tm_n, strip_n),
        out_shape=(
            pltpu.VMEM((frames, factors), BF16),
            pltpu.VMEM((frames, pixels), BF16),
            pltpu.VMEM((factors, pixels), BF16),
            pltpu.VMEM((per, frames), F32),
        ),
        in_specs=[hbm] * 7,
        out_specs=(vmem,) * 4,
        scratch_shapes=[
            pltpu.VMEM((frames, pixels), BF16),
            pltpu.VMEM((pixels, factors), BF16),
            pltpu.VMEM((2, frames, cols), BF16),
            pltpu.VMEM((rows, frames, 128), F32),
            pltpu.VMEM((rows, frames), F32),
            pltpu.VMEM((tm_n, frames), F32),
            pltpu.VMEM((tm_n, frames), F32),
            pltpu.VMEM((1, factors), F32),
            pltpu.VMEM((2 * steps + 4, frames, 128), F32),
            pltpu.VMEM((4, tm_n, frames), F32),
            pltpu.VMEM((frames, factors), F32),
            pltpu.VMEM((frames, factors), F32),
            pltpu.VMEM((frames, factors), F32),
            pltpu.VMEM((2, 2 * halves, Z * CORES, 128), F32),
            pltpu.VMEM((frames, factors), F32),
            pltpu.VMEM((strip_n, share, factors), BF16),
            pltpu.VMEM((frames, factors), BF16),
            pltpu.VMEM((Z * CORES, 2 * halves, 128), F32),
            pltpu.VMEM((2 * strip_n, 2 * halves, 128), F32),
            pltpu.VMEM((factors, frames), F32),
            DMA((7,)), DMA((2,)), DMA((2,)),
            DMA((8,)),
            pltpu.VMEM((2 * halves, 128), F32),
            pltpu.VMEM((frames, factors), BF16),
            pltpu.VMEM((2, 2 * halves, 128), F32),
            pltpu.VMEM((2 * halves, tm_n, 128), F32),
            pltpu.SemaphoreType.REGULAR((ROUNDS,)),
        ],
        compiler_params=pltpu.CompilerParams(
            collective_id=0, has_side_effects=True, vmem_limit_bytes=32 << 20
        ),
    )(
        *(
            pltpu.with_memory_space_constraint(x, pltpu.HBM)
            for x in (
                movie, shifts.T, projection, footprints,
                quality.reshape(tm_n, frames), continuity.reshape(tm_n, frames),
                retention.reshape(1, factors),
            )
        )
    )
    return pl.pallas_call(
        rebuild,
        out_shape=(
            jax.ShapeDtypeStruct((per, frames), F32),
            jax.ShapeDtypeStruct((frames, pixels), BF16),
        ),
        in_specs=[vmem] * 4,
        out_specs=(hbm, hbm),
        scratch_shapes=[pltpu.VMEM((frames, pixels), BF16), DMA((1 + pixels // 512,))],
        compiler_params=pltpu.CompilerParams(vmem_limit_bytes=16 << 20),
    )(low, warped, foot, act)


def solution(mesh):
    return jax.shard_map(
        functools.partial(body, mesh.shape["tm"], mesh.shape["strip"]),
        mesh=mesh,
        in_specs=(
            P("tm", "strip"), P("tm", "strip"), P("strip", None), P(None, "strip"), P(), P(), P(),
        ),
        out_specs=(P("strip", "tm"), P("tm", "strip")),
        check_vma=False,
    )
```
